32 devices in a mesh: cfg: 2 (over y), src: 4 (over z), col: 2 (over x), half: 2 (over core).
Axes of the slice: x: 2, y: 2, z: 4, core: 2. Of those that a mesh axis runs over, the one named last changes fastest.
Arguments:
- perambulator: bfloat16 [8, 4, 2, 512, 512], P(('cfg', 'src'), None, None, ('col', 'half')), parts along dimension 0, may hold values from -0.25 to 0.25
- elemental: bfloat16 [1, 8, 2, 128, 128], P(None, ('cfg', 'src')), parts along dimension 1, may hold values from -0.5 to 0.5
- source_order: int32 [8], P('cfg'), parts along dimension 0, may hold values from 0 to 3, as said below
- column_order: int32 [8, 128], P(('cfg', 'src')), parts along dimension 0, may hold values from 0 to 127, each once within a row
Outputs:
- meson_matrix: float32 [8, 2, 1, 1, 4], P(('cfg', 'src')), parts along dimension 0
The draws below stay inside these ranges and needn't reach their ends.
There are 2 independent parts, one for each index of `cfg`. The reference program is written for one: setup_inputs(seed, part) draws one part's arguments, and reference() takes and returns one part's arrays. A program takes and returns all parts, laid end to end along the dimension named above; each array names one. Nothing has to cross between parts.
Inputs may be any that keep to these rules, and one draw needn't show every extreme that they name: `source_order`: each of 0 to 3 appears once. `column_order`: each row holds each of 0 to 127 once.
All inputs are finite; a program needn't handle non-finite values.
Results may differ from the reference program's by a relative error of at most 0.0042.
Values may be sent and summed in bfloat16 or wider, within the bound.
A program may use at most 128 MiB of HBM per device.

```python
import jax
import jax.numpy as jnp
from jax import lax

NEV = 128
NOP = 1
DIM = 512
NT = 4


def draw_source_order(key, part):
    shuffled = jax.random.permutation(jax.random.fold_in(key, 11), NT).astype(jnp.int32)
    target = (jnp.asarray(part, jnp.int32) % NT).astype(jnp.int32)
    where_target = jnp.argmax((shuffled == target).astype(jnp.int32)).astype(jnp.int32)
    first_value = shuffled[0]
    swapped = shuffled.at[where_target].set(first_value)
    return swapped.at[0].set(target)


def shard_levels(own_key, dims, shards, least, largest):
    level, own = 1.0, jax.random.fold_in(own_key, 6)
    for dim, blocks in shards:
        steps = jnp.exp(jax.random.uniform(jax.random.fold_in(own, dim), (blocks,), jnp.float32, least / len(shards), largest / len(shards)))
        level = level * jnp.repeat(steps, dims[dim] // blocks).reshape([-1 if axis == dim else 1 for axis in range(len(dims))])
    return level


def gaussian(own_key, shape, width, bound, cuts=(), kind=jnp.bfloat16):
    entries = width * jax.random.normal(own_key, shape, jnp.float32)
    if cuts:
        entries = entries * shard_levels(own_key, shape, cuts, -0.22, 0.18)
    return jnp.clip(entries, -bound, bound).astype(kind)


def setup_inputs(seed: int = 0, part: int = 0) -> dict:
    key_list = jax.random.split(jax.random.key(seed), 5)
    own_keys = jax.random.split(jax.random.fold_in(key_list[4], part), 5)
    perambulator = gaussian(own_keys[0], (NT, NT, 2, DIM, DIM), (DIM ** -0.5), 0.25, ((0, 4), (3, 4)))
    elemental = gaussian(own_keys[1], (NOP, NT, 2, NEV, NEV), NEV ** -0.5, 0.5, ((1, 4),))
    source_order = draw_source_order(jax.random.fold_in(jax.random.fold_in(key_list[4], part), 71), part)
    column_order = jax.vmap(lambda own: jax.random.permutation(own, NEV))(jax.random.split(own_keys[3], NT)).reshape((NT, NEV)).astype(jnp.int32)
    return dict(perambulator=perambulator, elemental=elemental, source_order=source_order, column_order=column_order)


spin_sign = (1.0, 1.0, -1.0, -1.0)


def apply_rows(coefficients, tiles):
    slot_count = tiles.shape[0]
    column_count = tiles.shape[2]
    coef_real = coefficients[:, :, 0].astype(jnp.float32)
    coef_imag = coefficients[:, :, 1].astype(jnp.float32)
    tile_view = tiles.astype(jnp.float32).reshape(slot_count, 2, column_count, 4, NEV)
    tile_real = tile_view[:, 0]
    tile_imag = tile_view[:, 1]
    form = "qomr,qjsr->qosmj"
    highest = lax.Precision.HIGHEST
    real_part = jnp.einsum(form, coef_real, tile_real, precision=highest) - jnp.einsum(form, coef_imag, tile_imag, precision=highest)
    imag_part = jnp.einsum(form, coef_real, tile_imag, precision=highest) + jnp.einsum(form, coef_imag, tile_real, precision=highest)
    sign_table = jnp.array(spin_sign, jnp.float32)[:, None, None]
    stacked = jnp.stack([real_part * sign_table, imag_part * sign_table], axis=2)
    return stacked.reshape(slot_count, coefficients.shape[1], 2, 4 * NEV, column_count).astype(jnp.bfloat16)


def reference(perambulator, elemental, source_order, column_order):
    reordered = jax.vmap(lambda matrices, ordering: matrices[:, :, ordering, :], in_axes=(1, 0), out_axes=1)(elemental, column_order)
    by_slot = jnp.moveaxis(reordered, 1, 0)

    def one_source(slot):
        forward = apply_rows(by_slot, jnp.take(perambulator[slot], source_order, axis=0))
        own_coef = jnp.broadcast_to(by_slot[slot], by_slot.shape)
        backward = apply_rows(own_coef, jnp.take(perambulator, source_order[slot], axis=1))
        pair_sums = jnp.einsum("qaxij,qbyji->qabxy", forward.astype(jnp.float32), backward.astype(jnp.float32), precision=lax.Precision.HIGHEST)
        real_part = pair_sums[..., 0, 0] - pair_sums[..., 1, 1]
        imag_part = pair_sums[..., 0, 1] + pair_sums[..., 1, 0]
        return jnp.transpose(jnp.stack([real_part, imag_part], 0), (0, 2, 3, 1))

    return lax.map(one_source, jnp.arange(NT, dtype=jnp.int32))
```

```python
import functools

import jax
import jax.numpy as jnp
from jax import lax
from jax.experimental import pallas as pl
from jax.experimental.pallas import tpu as pltpu
from jax.sharding import PartitionSpec as P

spin_sign = (1.0, 1.0, -1.0, -1.0)
MESH = pl.DeviceIdType.MESH
NT = (((1,), (1,)), ((), ()))


def dot_nt(a, b):
    return lax.dot_general(a, b, NT, preferred_element_type=jnp.float32)


def sends(source, target):
    even = lax.rem(source + target, 2) == 0
    return jnp.logical_and(even, source < target) | jnp.logical_and(
        jnp.logical_not(even), source > target
    )


def kernel(
    sizes,
    tiles_hbm, elem_hbm, order_hbm, column_hbm,
    out_ref,
    tiles, elem, order, column,
    sorted_tiles, coef, mirror, result,
    load_sem, tile_send, tile_recv, coef_send, coef_recv, share_send, share_recv,
    result_send, result_recv, above, below,
):
    src_count, col_count, half_count = sizes
    blocks = col_count * half_count
    block_cols, components = tiles.shape[2], tiles.shape[3]
    eigen = elem.shape[-1]
    spins = components // eigen
    piece = eigen // blocks
    p = lax.axis_index("src")
    b = lax.axis_index("col") * half_count + lax.axis_index("half")

    def device(slot, block):
        return {
            "src": slot,
            "col": lax.div(block, half_count),
            "half": lax.rem(block, half_count),
        }

    def wait_bytes(ref, sem):
        pltpu.make_async_copy(ref, ref, sem).wait()

    barrier = pltpu.get_barrier_semaphore()

    def signal(sem, slot, block):
        pl.semaphore_signal(
            sem, inc=1, device_id=device(slot, block), device_id_type=MESH
        )

    @pl.when(p < src_count - 1)
    def _():
        for k in range(blocks):
            signal(barrier, p + 1, k)

    loads = [
        pltpu.make_async_copy(order_hbm, order, load_sem.at[0]),
        pltpu.make_async_copy(tiles_hbm.at[0], tiles, load_sem.at[1]),
        pltpu.make_async_copy(elem_hbm.at[0, 0], elem, load_sem.at[2]),
        pltpu.make_async_copy(column_hbm, column, load_sem.at[3]),
    ]
    for load in loads:
        load.start()

    @pl.when(p > 0)
    def _():
        pl.semaphore_wait(barrier, blocks)
        for k in range(blocks):
            signal(above.at[p], p - 1, k)

    @pl.when(p < src_count - 1)
    def _():
        pl.semaphore_wait(above.at[p + 1], blocks)

        @pl.when(p > 0)
        def _():
            signal(above.at[p + 1], p - 1, b)

    @pl.when(p > 0)
    def _():
        @pl.when(p > 1)
        def _():
            pl.semaphore_wait(below, 1)

    @pl.when(jnp.logical_and(p > 0, p < src_count - 1))
    def _():
        signal(below, p + 1, b)

    @pl.loop(0, src_count)
    def _(slot):
        @pl.when(slot > p + 1)
        def _():
            pl.semaphore_wait(above.at[slot], 1)

            @pl.when(p > 0)
            def _():
                signal(above.at[slot], p - 1, b)

    loads[2].wait()
    loads[3].wait()
    pick = (
        lax.broadcasted_iota(jnp.int32, (eigen, eigen), 0) == column[...]
    ).astype(jnp.float32).T.astype(jnp.bfloat16)
    both = jnp.concatenate([elem[0], elem[1]], axis=1)
    rows = jnp.dot(pick, both, preferred_element_type=jnp.float32).astype(jnp.bfloat16)
    coef[p, 0] = rows[:, :eigen]
    coef[p, 1] = rows[:, eigen:]

    loads[0].wait()
    loads[1].wait()

    @pl.loop(0, src_count)
    def _(slot):
        sorted_tiles[slot] = tiles[order[slot]]

    my_spin = lax.div(b * block_cols, eigen)
    my_lanes = pl.ds(pl.multiple_of(my_spin * eigen, eigen), eigen)
    my_rows = pl.ds(pl.multiple_of(b * block_cols, block_cols), block_cols)
    mirror[p, :, my_rows, :] = sorted_tiles[p, :, :, my_lanes]

    def partner(step):
        distance = 1 + lax.div(step, 2)
        slot = jnp.where(lax.rem(step, 2) == 0, p + distance, p - distance)
        valid = jnp.logical_and(slot >= 0, slot < src_count)
        return jnp.clip(slot, 0, src_count - 1), valid

    my_piece = pl.ds(pl.multiple_of(b * piece, piece), piece)

    def send_tile(slot, block):
        lanes = pl.ds(pl.multiple_of(lax.div(block * block_cols, eigen) * eigen, eigen), eigen)
        pltpu.make_async_remote_copy(
            src_ref=sorted_tiles.at[slot, :, :, lanes],
            dst_ref=mirror.at[p, :, my_rows, :],
            send_sem=tile_send.at[slot],
            recv_sem=tile_recv.at[p],
            device_id=device(slot, block),
            device_id_type=MESH,
        ).start()

    steps = 2 * (src_count - 1)

    @pl.loop(0, steps)
    def _(step):
        slot, valid = partner(step)

        @pl.when(jnp.logical_and(valid, sends(p, slot)))
        def _():
            pltpu.make_async_remote_copy(
                src_ref=coef.at[p, :, my_piece, :],
                dst_ref=coef.at[p, :, my_piece, :],
                send_sem=coef_send.at[slot],
                recv_sem=coef_recv.at[p],
                device_id={"src": slot},
                device_id_type=MESH,
            ).start()

    @pl.loop(0, steps)
    def _(step):
        slot, valid = partner(step)

        @pl.when(jnp.logical_and(valid, sends(p, slot)))
        def _():
            @pl.loop(0, blocks)
            def _(k):
                send_tile(slot, lax.rem(b + k, blocks))

    @pl.loop(1, blocks)
    def _(k):
        send_tile(p, lax.rem(b + k, blocks))

    @pl.loop(0, steps)
    def _(step):
        slot, valid = partner(step)

        @pl.when(jnp.logical_and(valid, sends(slot, p)))
        def _():
            wait_bytes(coef.at[slot, :, pl.ds(0, piece), :], coef_recv.at[slot])

            @pl.loop(1, blocks)
            def _(k):
                pltpu.make_async_remote_copy(
                    src_ref=coef.at[slot, :, my_piece, :],
                    dst_ref=coef.at[slot, :, my_piece, :],
                    send_sem=share_send.at[slot],
                    recv_sem=share_recv.at[slot],
                    device_id=device(p, lax.rem(b + k, blocks)),
                    device_id_type=MESH,
                ).start()

    def fold(value):
        return jnp.sum(value.reshape(block_cols // 8, 8, eigen), axis=0)

    offset = pl.ds(pl.multiple_of(lax.rem(b * block_cols, eigen), block_cols), block_cols)
    own_sign = jnp.where(my_spin < 2, spin_sign[0], spin_sign[2]).astype(jnp.float32)

    def pair(slot):
        own_real, own_imag = coef[p, 0, offset, :], coef[p, 1, offset, :]
        left = jnp.concatenate(
            [
                jnp.concatenate([own_real, -own_imag], axis=1),
                jnp.concatenate([own_imag, own_real], axis=1),
            ],
            axis=0,
        )
        far_real, far_imag = coef[slot, 0], coef[slot, 1]
        right = jnp.concatenate(
            [
                jnp.concatenate([far_real, -far_imag], axis=1),
                jnp.concatenate([far_imag, far_real], axis=1),
            ],
            axis=0,
        )
        total_real = jnp.zeros((8, eigen), jnp.float32)
        total_imag = jnp.zeros((8, eigen), jnp.float32)
        for spin in range(spins):
            part = slice(spin * eigen, (spin + 1) * eigen)
            near = jnp.concatenate(
                [sorted_tiles[slot, 0, :, part], sorted_tiles[slot, 1, :, part]], axis=1
            )
            away = jnp.concatenate([mirror[slot, 0, part, :], mirror[slot, 1, part, :]], axis=1)
            forward = dot_nt(near, right).astype(jnp.bfloat16).astype(jnp.float32)
            backward = dot_nt(left, away).astype(jnp.bfloat16).astype(jnp.float32)
            fr, fi = forward[:, :eigen], forward[:, eigen:]
            br, bi = backward[:block_cols], backward[block_cols:]
            total_real += spin_sign[spin] * fold(fr * br - fi * bi)
            total_imag += spin_sign[spin] * fold(fr * bi + fi * br)
        result[slot, b, 0] = own_sign * total_real
        result[slot, b, 1] = own_sign * total_imag

    def send_result(slot, target, block, there):
        pltpu.make_async_remote_copy(
            src_ref=result.at[slot, b],
            dst_ref=result.at[there, b],
            send_sem=result_send.at[slot],
            recv_sem=result_recv.at[there],
            device_id=device(target, block),
            device_id_type=MESH,
        ).start()

    def share_in_slot(slot):
        @pl.loop(1, blocks)
        def _(k):
            send_result(slot, p, lax.rem(b + k, blocks), slot)

    wait_bytes(mirror.at[p, :, pl.ds(0, components - block_cols), :], tile_recv.at[p])
    pair(p)
    share_in_slot(p)

    @pl.loop(0, steps)
    def _(step):
        slot, valid = partner(step)

        @pl.when(jnp.logical_and(valid, sends(slot, p)))
        def _():
            wait_bytes(coef.at[slot, :, pl.ds(0, eigen - piece), :], share_recv.at[slot])
            wait_bytes(mirror.at[slot], tile_recv.at[slot])
            pair(slot)

            @pl.loop(0, blocks)
            def _(k):
                send_result(slot, slot, lax.rem(b + k, blocks), p)

            share_in_slot(slot)

    wait_bytes(mirror.at[p, :, pl.ds(0, components - block_cols), :], tile_send.at[p])
    wait_bytes(result.at[p, pl.ds(0, blocks - 1)], result_send.at[p])

    @pl.loop(0, steps)
    def _(step):
        slot, valid = partner(step)

        @pl.when(jnp.logical_and(valid, sends(p, slot)))
        def _():
            wait_bytes(coef.at[slot, :, pl.ds(0, piece), :], coef_send.at[slot])
            wait_bytes(mirror.at[slot], tile_send.at[slot])

        @pl.when(jnp.logical_and(valid, sends(slot, p)))
        def _():
            wait_bytes(coef.at[slot, :, pl.ds(0, eigen - piece), :], share_send.at[slot])
            wait_bytes(result.at[slot], result_send.at[slot])
            wait_bytes(result.at[slot, pl.ds(0, blocks - 1)], result_send.at[slot])

    @pl.loop(0, src_count)
    def _(slot):
        here = jnp.logical_or(slot == p, sends(slot, p))

        @pl.when(here)
        def _():
            wait_bytes(result.at[slot, pl.ds(0, blocks - 1)], result_recv.at[slot])

        @pl.when(jnp.logical_not(here))
        def _():
            wait_bytes(result.at[slot], result_recv.at[slot])

    lane = lax.broadcasted_iota(jnp.int32, (1, src_count), 1)
    rows = [jnp.zeros((1, src_count), jnp.float32)] * 2
    for slot in range(src_count):
        total = jnp.sum(result[slot], axis=0)
        for part in (0, 1):
            rows[part] = jnp.where(lane == slot, jnp.sum(total[part], keepdims=True), rows[part])
    out_ref[0, 0, 0] = rows[0]
    out_ref[0, 1, 0] = rows[1]


def on_device(sizes, perambulator, elemental, source_order, column_order):
    operators = elemental.shape[0]
    eigen = elemental.shape[-1]
    _, slots, _, block_cols, components = perambulator.shape
    src_count, col_count, half_count = sizes
    blocks = col_count * half_count
    sem = pltpu.SemaphoreType.DMA
    return pl.pallas_call(
        functools.partial(kernel, sizes),
        out_shape=pltpu.VMEM((1, 2, operators, operators, slots), jnp.float32),
        in_specs=[pl.BlockSpec(memory_space=pl.ANY)] * 4,
        out_specs=pl.BlockSpec(memory_space=pltpu.VMEM),
        scratch_shapes=[
            pltpu.VMEM((slots, 2, block_cols, components), jnp.bfloat16),
            pltpu.VMEM((2, eigen, eigen), jnp.bfloat16),
            pltpu.SMEM((slots,), jnp.int32),
            pltpu.VMEM((1, eigen), jnp.int32),
            pltpu.VMEM((slots, 2, block_cols, components), jnp.bfloat16),
            pltpu.VMEM((slots, 2, eigen, eigen), jnp.bfloat16),
            pltpu.VMEM((slots, 2, components, eigen), jnp.bfloat16),
            pltpu.VMEM((slots, blocks, 2, 8, eigen), jnp.float32),
            sem((4,)),
        ]
        + [sem((slots,))] * 8
        + [pltpu.SemaphoreType.REGULAR((slots,)), pltpu.SemaphoreType.REGULAR],
        compiler_params=pltpu.CompilerParams(collective_id=0, has_side_effects=True),
    )(perambulator, elemental, source_order, column_order)


def solution(mesh):
    sizes = (mesh.shape["src"], mesh.shape["col"], mesh.shape["half"])
    return jax.shard_map(
        functools.partial(on_device, sizes),
        mesh=mesh,
        in_specs=(
            P(("cfg", "src"), None, None, ("col", "half"), None),
            P(None, ("cfg", "src"), None, None, None),
            P("cfg"),
            P(("cfg", "src"), None),
        ),
        out_specs=P(("cfg", "src"), None, None, None, None),
        check_vma=False,
    )
```

```python
import functools

import jax
import jax.numpy as jnp
from jax import lax
from jax.experimental import pallas as pl
from jax.experimental.pallas import tpu as pltpu
from jax.sharding import PartitionSpec as P

spin_sign = (1.0, 1.0, -1.0, -1.0)
MESH = pl.DeviceIdType.MESH
NT = (((1,), (1,)), ((), ()))


def dot_nt(a, b):
    return lax.dot_general(a, b, NT, preferred_element_type=jnp.float32)


def kernel(
    sizes,
    tiles_hbm, elem_hbm, order_hbm, column_hbm,
    out_ref,
    tiles, elem, order, column,
    near, coef, left, mirror, forward, partial, result, total,
    load_sem, tile_send, tile_recv, coef_send, coef_recv, share_send, share_recv,
    diag_send, diag_recv, result_send, result_recv, above, below,
):
    src_count, col_count, half_count = sizes
    blocks = col_count * half_count
    half = blocks // 2
    block_cols, components = tiles.shape[2], tiles.shape[3]
    eigen = elem.shape[-1]
    spins = components // eigen
    piece = eigen // blocks
    last = src_count - 1
    p = lax.axis_index("src")
    b = lax.axis_index("col") * half_count + lax.axis_index("half")
    offsets = [2 * j if j < half else 2 * (j - half) + 1 for j in range(blocks)]
    each = functools.partial(pl.loop, unroll=src_count <= 8)

    def device(slot, block):
        return {
            "src": slot,
            "col": lax.div(block, half_count),
            "half": lax.rem(block, half_count),
        }

    def signal(sem, slot, block):
        pl.semaphore_signal(sem, inc=1, device_id=device(slot, block), device_id_type=MESH)

    def send(src, dst, send_sem, recv_sem, slot, block):
        pltpu.make_async_remote_copy(
            src_ref=src, dst_ref=dst, send_sem=send_sem, recv_sem=recv_sem,
            device_id=device(slot, block), device_id_type=MESH,
        ).start()

    def wait_bytes(ref, sem):
        pltpu.make_async_copy(ref, ref, sem).wait()

    def shifted(block, offset):
        return lax.rem(block + offset + blocks, blocks)

    def spin_of(block):
        return lax.div(block * block_cols, eigen)

    def sign_of(block):
        return jnp.where(spin_of(block) < 2, spin_sign[0], spin_sign[2]).astype(jnp.float32)

    def rows_of(block):
        return pl.ds(pl.multiple_of(lax.rem(block * block_cols, eigen), block_cols), block_cols)

    def upward(low, high):
        distance = high - low
        whole = jnp.where(lax.rem(distance, 2) == 0, blocks, 0)
        return jnp.where(jnp.logical_and(low == 0, distance > 1), whole, half)

    def count(source, target):
        n = upward(jnp.minimum(source, target), jnp.maximum(source, target))
        return jnp.where(source < target, n, blocks - n)

    def goes(source, target, j):
        n = upward(jnp.minimum(source, target), jnp.maximum(source, target))
        return jnp.where(source < target, j < n, j >= n)

    barrier = pltpu.get_barrier_semaphore()

    @pl.when(p < last)
    def _():
        for k in range(blocks):
            signal(barrier, p + 1, k)

    loads = [
        pltpu.make_async_copy(elem_hbm.at[0, 0], elem, load_sem.at[0]),
        pltpu.make_async_copy(column_hbm, column, load_sem.at[1]),
        pltpu.make_async_copy(order_hbm, order, load_sem.at[2]),
        pltpu.make_async_copy(tiles_hbm.at[0], tiles, load_sem.at[3]),
    ]
    for load in loads:
        load.start()

    @pl.when(p > 0)
    def _():
        pl.semaphore_wait(barrier, blocks)
        for k in range(blocks):
            signal(above.at[p], p - 1, k)

    loads[0].wait()
    loads[1].wait()
    pick = (
        lax.broadcasted_iota(jnp.int32, (eigen, eigen), 0) == column[...]
    ).astype(jnp.float32).T.astype(jnp.bfloat16)
    both = jnp.concatenate([elem[0], elem[1]], axis=1)
    picked = jnp.dot(pick, both, preferred_element_type=jnp.float32).astype(jnp.bfloat16)
    coef[p, 0] = picked[:, :eigen]
    coef[p, 1] = picked[:, eigen:]

    loads[2].wait()
    loads[3].wait()

    @each(0, src_count)
    def _(slot):
        for spin in range(spins):
            near[slot, spin] = tiles[order[slot], :, :, spin * eigen : (spin + 1) * eigen]

    my_piece = pl.ds(pl.multiple_of(b * piece, piece), piece)

    def send_coef(slot):
        @pl.when(count(p, slot) > 0)
        def _():
            send(
                coef.at[p, :, my_piece, :], coef.at[p, :, my_piece, :],
                coef_send.at[slot], coef_recv.at[p], slot, b,
            )

    def send_unit(slot, j):
        @pl.when(goes(p, slot, j))
        def _():
            block = jnp.where(p < slot, shifted(b, offsets[j]), shifted(b, -offsets[j]))
            send(
                near.at[slot, spin_of(block)], mirror.at[p, b],
                tile_send.at[slot], tile_recv.at[p, b], slot, block,
            )

    def send_far(slot):
        send_coef(slot)
        for j in range(blocks):
            send_unit(slot, j)

    @pl.when(p > 0)
    def _():
        send_coef(p - 1)
        send_unit(p - 1, half)

    @pl.when(p < last)
    def _():
        pl.semaphore_wait(above.at[p + 1], blocks)

        @pl.when(p > 0)
        def _():
            signal(above.at[p + 1], p - 1, b)

        @pl.when(p < 2)
        def _():
            signal(below, p + 1, b)

        send_coef(p + 1)
        send_unit(p + 1, 0)

    @each(0, src_count)
    def _(slot):
        @pl.when(slot > p + 1)
        def _():
            pl.semaphore_wait(above.at[slot], 1)

            @pl.when(p > 0)
            def _():
                signal(above.at[slot], p - 1, b)

            send_far(slot)

    @pl.when(p > 0)
    def _():
        pl.semaphore_wait(below, 1)

        @pl.when(jnp.logical_and(p > 1, p < last))
        def _():
            signal(below, p + 1, b)

    @each(0, src_count)
    def _(slot):
        @pl.when(slot < p - 1)
        def _():
            send_far(slot)

    @pl.when(p < last)
    def _():
        for j in range(1, half):
            send_unit(p + 1, j)

    @pl.when(p > 0)
    def _():
        for j in range(half + 1, blocks):
            send_unit(p - 1, j)

    def diag_source(k):
        return b >= half if k == half else b >= 0

    def diag_target(k):
        return b < half if k == half else b >= 0

    for k in range(1, half + 1):
        @pl.when(diag_source(k))
        def _():
            block = shifted(b, -k)
            send(
                near.at[p, spin_of(block)], mirror.at[p, b],
                diag_send.at[k], diag_recv.at[k], p, block,
            )

    own_real, own_imag = coef[p, 0, rows_of(b), :], coef[p, 1, rows_of(b), :]
    left[:block_cols, :eigen] = own_real
    left[:block_cols, eigen:] = -own_imag
    left[block_cols:, :eigen] = own_imag
    left[block_cols:, eigen:] = own_real

    def make_forward(slot, block):
        far_real, far_imag = coef[slot, 0, rows_of(block), :], coef[slot, 1, rows_of(block), :]
        mine = jnp.concatenate([near[slot, spin_of(block), 0], near[slot, spin_of(block), 1]], axis=1)
        real = jnp.concatenate([far_real, -far_imag], axis=1)
        imag = jnp.concatenate([far_imag, far_real], axis=1)
        forward[slot, block, 0] = dot_nt(mine, real).astype(jnp.bfloat16)
        forward[slot, block, 1] = dot_nt(mine, imag).astype(jnp.bfloat16)

    def fold(value):
        return jnp.sum(value.reshape(block_cols // 8, 8, block_cols), axis=0)

    def multiply(slot, block, away, weight, first):
        backward = dot_nt(left[...], jnp.concatenate([away[0], away[1]], axis=1))
        backward = backward.astype(jnp.bfloat16).astype(jnp.float32)
        br, bi = backward[:block_cols], backward[block_cols:]
        fr = forward[slot, block, 0].astype(jnp.float32)
        fi = forward[slot, block, 1].astype(jnp.float32)
        scale = weight * sign_of(block) * sign_of(b)
        real = scale * fold(fr * br - fi * bi)
        imag = scale * fold(fr * bi + fi * br)
        packed = jnp.concatenate([real[:4] + real[4:], imag[:4] + imag[4:]], axis=0)
        if first:
            partial[slot] = packed
        else:
            partial[slot] += packed

    def share_result(slot):
        result[slot, 0, b] = partial[slot]
        for k in range(1, blocks):
            block = shifted(b, k)
            send(
                result.at[slot, 0, b], result.at[slot, 0, b],
                result_send.at[slot], result_recv.at[slot, 0], p, block,
            )

    def send_result(slot):
        for k in range(blocks):
            block = shifted(b, k)
            send(
                result.at[slot, 0, b], result.at[p, 1, b],
                result_send.at[slot], result_recv.at[p, 1], slot, block,
            )

    @each(0, src_count)
    def _(slot):
        @pl.when(jnp.logical_and(slot != p, count(slot, p) > 0))
        def _():
            wait_bytes(coef.at[slot, :, pl.ds(0, piece), :], coef_recv.at[slot])
            for k in range(1, blocks):
                send(
                    coef.at[slot, :, my_piece, :], coef.at[slot, :, my_piece, :],
                    share_send.at[slot], share_recv.at[slot], p, shifted(b, k),
                )

    make_forward(p, b)
    multiply(p, b, near[p, spin_of(b)], 1.0, True)
    for k in range(1, half + 1):
        @pl.when(diag_target(k))
        def _():
            block = shifted(b, k)
            make_forward(p, block)
            wait_bytes(mirror.at[p, block], diag_recv.at[k])
            multiply(p, block, mirror[p, block], 2.0, False)
    share_result(p)

    def source_block(slot, j):
        return jnp.where(slot < p, shifted(b, -offsets[j]), shifted(b, offsets[j]))

    @each(0, src_count)
    def _(slot):
        @pl.when(jnp.logical_and(slot != p, count(slot, p) > 0))
        def _():
            wait_bytes(coef.at[slot, :, pl.ds(0, eigen - piece), :], share_recv.at[slot])
            partial[slot] = jnp.zeros(partial.shape[1:], jnp.float32)
            for j in range(blocks):
                @pl.when(goes(slot, p, j))
                def _():
                    make_forward(slot, source_block(slot, j))

    def take_unit(slot, j):
        @pl.when(goes(slot, p, j))
        def _():
            block = source_block(slot, j)
            wait_bytes(mirror.at[slot, block], tile_recv.at[slot, block])
            multiply(slot, block, mirror[slot, block], 1.0, False)

    def finish(slot):
        @pl.when(count(slot, p) > 0)
        def _():
            share_result(slot)
            send_result(slot)

    @pl.when(p > 0)
    def _():
        take_unit(p - 1, 0)

    @pl.when(p < last)
    def _():
        take_unit(p + 1, half)

    @each(0, src_count)
    def _(slot):
        @pl.when(jnp.logical_or(slot > p + 1, slot < p - 1))
        def _():
            for j in range(blocks):
                take_unit(slot, j)
            finish(slot)

    @pl.when(p > 0)
    def _():
        for j in range(1, half):
            take_unit(p - 1, j)
        finish(p - 1)

    @pl.when(p < last)
    def _():
        for j in range(half + 1, blocks):
            take_unit(p + 1, j)
        finish(p + 1)

    wait_bytes(result.at[p, 0, pl.ds(0, blocks - 1)], result_send.at[p])
    for k in range(1, half + 1):
        @pl.when(diag_source(k))
        def _():
            wait_bytes(mirror.at[p, 0], diag_send.at[k])

    @each(0, src_count)
    def _(slot):
        @pl.when(slot != p)
        def _():
            sent, received = count(p, slot), count(slot, p)

            @pl.when(sent > 0)
            def _():
                wait_bytes(coef.at[slot, :, pl.ds(0, piece), :], coef_send.at[slot])

            @pl.when(sent == half)
            def _():
                wait_bytes(mirror.at[slot, pl.ds(0, half)], tile_send.at[slot])

            @pl.when(sent == blocks)
            def _():
                wait_bytes(mirror.at[slot], tile_send.at[slot])

            @pl.when(received > 0)
            def _():
                wait_bytes(coef.at[slot, :, pl.ds(0, eigen - piece), :], share_send.at[slot])
                wait_bytes(result.at[slot, 0], result_send.at[slot])
                wait_bytes(result.at[slot, 0, pl.ds(0, blocks - 1)], result_send.at[slot])

    @each(0, src_count)
    def _(slot):
        total[slot] = jnp.zeros(total.shape[1:], jnp.float32)

        @pl.when(jnp.logical_or(slot == p, count(slot, p) > 0))
        def _():
            wait_bytes(result.at[slot, 0, pl.ds(0, blocks - 1)], result_recv.at[slot, 0])
            total[slot] += jnp.sum(result[slot, 0], axis=0)

        @pl.when(jnp.logical_and(slot != p, count(p, slot) > 0))
        def _():
            wait_bytes(result.at[slot, 1], result_recv.at[slot, 1])
            total[slot] += jnp.sum(result[slot, 1], axis=0)

    lane = lax.broadcasted_iota(jnp.int32, (1, src_count), 1)
    rows = [jnp.zeros((1, src_count), jnp.float32)] * 2
    for slot in range(src_count):
        for part in (0, 1):
            value = jnp.sum(total[slot, 4 * part : 4 * part + 4], keepdims=True)
            rows[part] = jnp.where(lane == slot, value, rows[part])
    out_ref[0, 0, 0] = rows[0]
    out_ref[0, 1, 0] = rows[1]


def on_device(sizes, perambulator, elemental, source_order, column_order):
    operators = elemental.shape[0]
    eigen = elemental.shape[-1]
    _, slots, _, block_cols, components = perambulator.shape
    src_count, col_count, half_count = sizes
    blocks = col_count * half_count
    spins = components // eigen
    sem = pltpu.SemaphoreType.DMA
    flag = pltpu.SemaphoreType.REGULAR
    return pl.pallas_call(
        functools.partial(kernel, sizes),
        out_shape=pltpu.VMEM((1, 2, operators, operators, slots), jnp.float32),
        in_specs=[pl.BlockSpec(memory_space=pl.ANY)] * 4,
        out_specs=pl.BlockSpec(memory_space=pltpu.VMEM),
        scratch_shapes=[
            pltpu.VMEM((slots, 2, block_cols, components), jnp.bfloat16),
            pltpu.VMEM((2, eigen, eigen), jnp.bfloat16),
            pltpu.SMEM((slots,), jnp.int32),
            pltpu.VMEM((1, eigen), jnp.int32),
            pltpu.VMEM((slots, spins, 2, block_cols, eigen), jnp.bfloat16),
            pltpu.VMEM((slots, 2, eigen, eigen), jnp.bfloat16),
            pltpu.VMEM((2 * block_cols, 2 * eigen), jnp.bfloat16),
            pltpu.VMEM((slots, blocks, 2, block_cols, eigen), jnp.bfloat16),
            pltpu.VMEM((slots, blocks, 2, block_cols, block_cols), jnp.bfloat16),
            pltpu.VMEM((slots, 8, block_cols), jnp.float32),
            pltpu.VMEM((slots, 2, blocks, 8, block_cols), jnp.float32),
            pltpu.VMEM((slots, 8, block_cols), jnp.float32),
            sem((4,)),
            sem((slots,)),
            sem((slots, blocks)),
            sem((slots,)),
            sem((slots,)),
            sem((slots,)),
            sem((slots,)),
            sem((blocks,)),
            sem((blocks,)),
            sem((slots,)),
            sem((slots, 2)),
            flag((slots,)),
            flag,
        ],
        compiler_params=pltpu.CompilerParams(collective_id=0, has_side_effects=True),
    )(perambulator, elemental, source_order, column_order)


def solution(mesh):
    sizes = (mesh.shape["src"], mesh.shape["col"], mesh.shape["half"])
    return jax.shard_map(
        functools.partial(on_device, sizes),
        mesh=mesh,
        in_specs=(
            P(("cfg", "src"), None, None, ("col", "half"), None),
            P(None, ("cfg", "src"), None, None, None),
            P("cfg"),
            P(("cfg", "src"), None),
        ),
        out_specs=P(("cfg", "src"), None, None, None, None),
        check_vma=False,
    )
```

```python
import functools

import jax
import jax.numpy as jnp
from jax import lax
from jax.experimental import pallas as pl
from jax.experimental.pallas import tpu as pltpu
from jax.sharding import PartitionSpec as P

spin_sign = (1.0, 1.0, -1.0, -1.0)
MESH = pl.DeviceIdType.MESH
NT = (((1,), (1,)), ((), ()))


def dot_nt(a, b):
    return lax.dot_general(a, b, NT, preferred_element_type=jnp.float32)


def kernel(
    sizes,
    tiles_hbm, elem_hbm, order_hbm, column_hbm,
    out_ref,
    tiles, elem, order, column,
    near, coef, left, mirror, forward, partial, result, total,
    load_sem, tile_send, tile_recv, coef_send, coef_recv, share_send, share_recv,
    diag_send, diag_recv, result_send, result_recv, above,
):
    src_count, col_count, half_count = sizes
    blocks = col_count * half_count
    half = blocks // 2
    block_cols, components = tiles.shape[2], tiles.shape[3]
    eigen = elem.shape[-1]
    spins = components // eigen
    piece = eigen // blocks
    last = src_count - 1
    p = lax.axis_index("src")
    b = lax.axis_index("col") * half_count + lax.axis_index("half")
    offsets = [2 * j if j < half else 2 * (j - half) + 1 for j in range(blocks)]
    each = functools.partial(pl.loop, unroll=src_count <= 8)

    def device(slot, block):
        return {
            "src": slot,
            "col": lax.div(block, half_count),
            "half": lax.rem(block, half_count),
        }

    def signal(sem, slot, block):
        pl.semaphore_signal(sem, inc=1, device_id=device(slot, block), device_id_type=MESH)

    def send(src, dst, send_sem, recv_sem, slot, block):
        pltpu.make_async_remote_copy(
            src_ref=src, dst_ref=dst, send_sem=send_sem, recv_sem=recv_sem,
            device_id=device(slot, block), device_id_type=MESH,
        ).start()

    def wait_bytes(ref, sem):
        pltpu.make_async_copy(ref, ref, sem).wait()

    def shifted(block, offset):
        return lax.rem(block + offset + blocks, blocks)

    def spin_of(block):
        if isinstance(block, int):
            return block * block_cols // eigen
        return lax.div(block * block_cols, eigen)

    def sign_of(block):
        return jnp.where(spin_of(block) < 2, spin_sign[0], spin_sign[2]).astype(jnp.float32)

    def rows_of(block):
        if isinstance(block, int):
            return pl.ds(block * block_cols % eigen, block_cols)
        return pl.ds(pl.multiple_of(lax.rem(block * block_cols, eigen), block_cols), block_cols)

    def upward(low, high):
        whole = jnp.where(jnp.logical_or(lax.rem(high, 2) == 0, high - low == 1), blocks, 0)
        return jnp.where(high == 1, half, whole)

    def count(source, target):
        n = upward(jnp.minimum(source, target), jnp.maximum(source, target))
        return jnp.where(source < target, n, blocks - n)

    def goes(source, target, j):
        n = upward(jnp.minimum(source, target), jnp.maximum(source, target))
        return jnp.where(source < target, j < n, j >= n)

    barrier = pltpu.get_barrier_semaphore()

    for k in range(1, blocks):
        signal(barrier, p, shifted(b, k))

    @each(0, src_count)
    def _(slot):
        @pl.when(slot > p)
        def _():
            for k in range(blocks):
                signal(barrier, slot, k)

    loads = [
        pltpu.make_async_copy(elem_hbm.at[0, 0], elem, load_sem.at[0]),
        pltpu.make_async_copy(column_hbm, column, load_sem.at[1]),
        pltpu.make_async_copy(order_hbm, order, load_sem.at[2]),
        pltpu.make_async_copy(tiles_hbm.at[0], tiles, load_sem.at[3]),
    ]
    for load in loads:
        load.start()

    pl.semaphore_wait(barrier, blocks - 1 + p * blocks)

    @each(0, src_count)
    def _(slot):
        @pl.when(slot < p)
        def _():
            signal(above.at[p], slot, b)

    loads[0].wait()
    loads[1].wait()
    pick = (
        lax.broadcasted_iota(jnp.int32, (eigen, eigen), 0) == column[...]
    ).astype(jnp.float32).T.astype(jnp.bfloat16)
    both = jnp.concatenate([elem[0], elem[1]], axis=1)
    picked = jnp.dot(pick, both, preferred_element_type=jnp.float32).astype(jnp.bfloat16)
    coef[p, 0] = picked[:, :eigen]
    coef[p, 1] = picked[:, eigen:]

    loads[2].wait()
    loads[3].wait()

    @each(0, src_count)
    def _(slot):
        for spin in range(spins):
            near[slot, spin] = tiles[order[slot], :, :, spin * eigen : (spin + 1) * eigen]

    my_piece = pl.ds(pl.multiple_of(b * piece, piece), piece)

    def send_coef(slot):
        @pl.when(count(p, slot) > 0)
        def _():
            send(
                coef.at[p, :, my_piece, :], coef.at[p, :, my_piece, :],
                coef_send.at[slot], coef_recv.at[p], slot, b,
            )

    def send_unit(slot, j):
        @pl.when(goes(p, slot, j))
        def _():
            offset = jnp.where(lax.rem(b, 2) == 0, offsets[j], offsets[j ^ 1])
            block = jnp.where(p < slot, shifted(b, offset), shifted(b, -offset))
            send(
                near.at[slot, spin_of(block)], mirror.at[p, b],
                tile_send.at[slot], tile_recv.at[p, b], slot, block,
            )

    def send_units(slot, start, stop):
        for j in range(start, stop):
            send_unit(slot, j)

    @each(0, src_count)
    def _(slot):
        @pl.when(slot < p)
        def _():
            send_coef(slot)

    @each(0, src_count)
    def _(slot):
        @pl.when(slot < p)
        def _():
            send_units(slot, 0, blocks)

    @pl.when(p < last)
    def _():
        pl.semaphore_wait(above.at[p + 1], 1)
        send_coef(p + 1)
        send_units(p + 1, 0, 1)

    @each(0, src_count)
    def _(slot):
        @pl.when(slot > p + 1)
        def _():
            pl.semaphore_wait(above.at[slot], 1)
            send_coef(slot)
            send_units(slot, 0, blocks)

    @pl.when(p < last)
    def _():
        send_units(p + 1, 1, blocks)

    def others(act):
        @each(0, src_count)
        def _(slot):
            @pl.when(slot != p)
            def _():
                act(slot)

    def share_coef(slot):
        @pl.when(count(slot, p) > 0)
        def _():
            wait_bytes(coef.at[slot, :, pl.ds(0, piece), :], coef_recv.at[slot])
            for k in range(1, blocks):
                send(
                    coef.at[slot, :, my_piece, :], coef.at[slot, :, my_piece, :],
                    share_send.at[slot], share_recv.at[slot], p, shifted(b, k),
                )

    def diag_source(k):
        return b >= half if k == half else b >= 0

    def diag_target(k):
        return b < half if k == half else b >= 0

    for k in range(1, half + 1):
        @pl.when(diag_source(k))
        def _():
            block = shifted(b, -k)
            send(
                near.at[p, spin_of(block)], mirror.at[p, b],
                diag_send.at[k], diag_recv.at[k], p, block,
            )

    own_real, own_imag = coef[p, 0, rows_of(b), :], coef[p, 1, rows_of(b), :]
    left[:block_cols, :eigen] = own_real
    left[:block_cols, eigen:] = -own_imag
    left[block_cols:, :eigen] = own_imag
    left[block_cols:, eigen:] = own_real

    def make_forward(slot, block):
        far_real, far_imag = coef[slot, 0, rows_of(block), :], coef[slot, 1, rows_of(block), :]
        mine = jnp.concatenate([near[slot, spin_of(block), 0], near[slot, spin_of(block), 1]], axis=1)
        real = jnp.concatenate([far_real, -far_imag], axis=1)
        imag = jnp.concatenate([far_imag, far_real], axis=1)
        product = dot_nt(jnp.concatenate([real, imag], axis=0), mine).astype(jnp.bfloat16)
        forward[slot, block, 0] = product[:block_cols]
        forward[slot, block, 1] = product[block_cols:]

    def fold(value):
        return jnp.sum(value.reshape(block_cols // 8, 8, block_cols), axis=0)

    def multiply(slot, block, away, weight, first):
        backward = dot_nt(jnp.concatenate([away[0], away[1]], axis=1), left[...])
        backward = backward.astype(jnp.bfloat16).astype(jnp.float32)
        br, bi = backward[:, :block_cols], backward[:, block_cols:]
        fr = forward[slot, block, 0].astype(jnp.float32)
        fi = forward[slot, block, 1].astype(jnp.float32)
        scale = weight * sign_of(block) * sign_of(b)
        real = scale * fold(fr * br - fi * bi)
        imag = scale * fold(fr * bi + fi * br)
        packed = jnp.concatenate([real[:4] + real[4:], imag[:4] + imag[4:]], axis=0)
        if first:
            partial[slot] = packed
        else:
            partial[slot] += packed

    def share_result(slot):
        result[slot, 0, b] = partial[slot]
        for k in range(1, blocks):
            block = shifted(b, k)
            send(
                result.at[slot, 0, b], result.at[slot, 0, b],
                result_send.at[slot], result_recv.at[slot, 0], p, block,
            )

    def send_result(slot):
        for k in range(blocks):
            block = shifted(b, k)
            send(
                result.at[slot, 0, b], result.at[p, 1, b],
                result_send.at[slot], result_recv.at[p, 1], slot, block,
            )

    make_forward(p, b)
    multiply(p, b, near[p, spin_of(b)], 1.0, True)
    for k in range(1, half + 1):
        @pl.when(diag_target(k))
        def _():
            make_forward(p, shifted(b, k))

    @each(0, src_count)
    def _(step):
        @pl.when(step < p)
        def _():
            share_coef(p - 1 - step)

    @each(0, src_count)
    def _(slot):
        @pl.when(slot > p)
        def _():
            share_coef(slot)


    def take_diagonal():
        for k in range(1, half + 1):
            @pl.when(diag_target(k))
            def _():
                block = shifted(b, k)
                wait_bytes(mirror.at[p, block], diag_recv.at[k])
                multiply(p, block, mirror[p, block], 2.0, False)
        share_result(p)

    def source_block(slot, j):
        return jnp.where(slot < p, shifted(b, -offsets[j]), shifted(b, offsets[j]))

    def prepare(slot):
        @pl.when(count(slot, p) > 0)
        def _():
            wait_bytes(coef.at[slot, :, pl.ds(0, eigen - piece), :], share_recv.at[slot])
            partial[slot] = jnp.zeros(partial.shape[1:], jnp.float32)
            for block in range(blocks):
                make_forward(slot, block)

    def take_units(slot, start, stop):
        @pl.when(goes(slot, p, start))
        def _():
            for j in range(start, stop):
                block = source_block(slot, j)
                wait_bytes(mirror.at[slot, block], tile_recv.at[slot, block])
            for j in range(start, stop):
                block = source_block(slot, j)
                multiply(slot, block, mirror[slot, block], 1.0, False)

    def finish(slot):
        @pl.when(count(slot, p) > 0)
        def _():
            share_result(slot)
            send_result(slot)

    def take_all(slot):
        take_units(slot, 0, half)
        take_units(slot, half, blocks)
        finish(slot)

    @each(0, src_count)
    def _(slot):
        @pl.when(slot != p)
        def _():
            prepare(slot)
            take_all(slot)

        @pl.when(slot == jnp.where(p == 0, 1, 0))
        def _():
            take_diagonal()

    for k in range(1, half + 1):
        @pl.when(diag_source(k))
        def _():
            wait_bytes(mirror.at[p, 0], diag_send.at[k])

    @each(0, src_count)
    def _(slot):
        @pl.when(slot != p)
        def _():
            sent, received = count(p, slot), count(slot, p)

            @pl.when(sent > 0)
            def _():
                wait_bytes(coef.at[slot, :, pl.ds(0, piece), :], coef_send.at[slot])

            for n in range(1, blocks + 1):
                @pl.when(sent == n)
                def _():
                    wait_bytes(mirror.at[slot, pl.ds(0, n)], tile_send.at[slot])

            @pl.when(received > 0)
            def _():
                wait_bytes(coef.at[slot, :, pl.ds(0, eigen - piece), :], share_send.at[slot])

    @each(0, src_count)
    def _(slot):
        total[slot] = jnp.zeros(total.shape[1:], jnp.float32)

        @pl.when(jnp.logical_or(slot == p, count(slot, p) > 0))
        def _():
            wait_bytes(result.at[slot, 0, pl.ds(0, blocks - 1)], result_recv.at[slot, 0])
            total[slot] += jnp.sum(result[slot, 0], axis=0)

        @pl.when(jnp.logical_and(slot != p, count(p, slot) > 0))
        def _():
            wait_bytes(result.at[slot, 1], result_recv.at[slot, 1])
            total[slot] += jnp.sum(result[slot, 1], axis=0)

    lane = lax.broadcasted_iota(jnp.int32, (1, src_count), 1)
    rows = [jnp.zeros((1, src_count), jnp.float32)] * 2
    for slot in range(src_count):
        for part in (0, 1):
            value = jnp.sum(total[slot, 4 * part : 4 * part + 4], keepdims=True)
            rows[part] = jnp.where(lane == slot, value, rows[part])
    out_ref[0, 0, 0] = rows[0]
    out_ref[0, 1, 0] = rows[1]

    wait_bytes(result.at[p, 0, pl.ds(0, blocks - 1)], result_send.at[p])

    @each(0, src_count)
    def _(slot):
        @pl.when(jnp.logical_and(slot != p, count(slot, p) > 0))
        def _():
            wait_bytes(result.at[slot, 0], result_send.at[slot])
            wait_bytes(result.at[slot, 0, pl.ds(0, blocks - 1)], result_send.at[slot])


def on_device(sizes, perambulator, elemental, source_order, column_order):
    operators = elemental.shape[0]
    eigen = elemental.shape[-1]
    _, slots, _, block_cols, components = perambulator.shape
    src_count, col_count, half_count = sizes
    blocks = col_count * half_count
    spins = components // eigen
    sem = pltpu.SemaphoreType.DMA
    flag = pltpu.SemaphoreType.REGULAR
    return pl.pallas_call(
        functools.partial(kernel, sizes),
        out_shape=pltpu.VMEM((1, 2, operators, operators, slots), jnp.float32),
        in_specs=[pl.BlockSpec(memory_space=pl.ANY)] * 4,
        out_specs=pl.BlockSpec(memory_space=pltpu.VMEM),
        scratch_shapes=[
            pltpu.VMEM((slots, 2, block_cols, components), jnp.bfloat16),
            pltpu.VMEM((2, eigen, eigen), jnp.bfloat16),
            pltpu.SMEM((slots,), jnp.int32),
            pltpu.VMEM((1, eigen), jnp.int32),
            pltpu.VMEM((slots, spins, 2, block_cols, eigen), jnp.bfloat16),
            pltpu.VMEM((slots, 2, eigen, eigen), jnp.bfloat16),
            pltpu.VMEM((2 * block_cols, 2 * eigen), jnp.bfloat16),
            pltpu.VMEM((slots, blocks, 2, block_cols, eigen), jnp.bfloat16),
            pltpu.VMEM((slots, blocks, 2, block_cols, block_cols), jnp.bfloat16),
            pltpu.VMEM((slots, 8, block_cols), jnp.float32),
            pltpu.VMEM((slots, 2, blocks, 8, block_cols), jnp.float32),
            pltpu.VMEM((slots, 8, block_cols), jnp.float32),
            sem((4,)),
            sem((slots,)),
            sem((slots, blocks)),
            sem((slots,)),
            sem((slots,)),
            sem((slots,)),
            sem((slots,)),
            sem((blocks,)),
            sem((blocks,)),
            sem((slots,)),
            sem((slots, 2)),
            flag((slots,)),
        ],
        compiler_params=pltpu.CompilerParams(collective_id=0, has_side_effects=True),
    )(perambulator, elemental, source_order, column_order)


def solution(mesh):
    sizes = (mesh.shape["src"], mesh.shape["col"], mesh.shape["half"])
    return jax.shard_map(
        functools.partial(on_device, sizes),
        mesh=mesh,
        in_specs=(
            P(("cfg", "src"), None, None, ("col", "half"), None),
            P(None, ("cfg", "src"), None, None, None),
            P("cfg"),
            P(("cfg", "src"), None),
        ),
        out_specs=P(("cfg", "src"), None, None, None, None),
        check_vma=False,
    )
```

```python
import functools

import jax
import jax.numpy as jnp
from jax import lax
from jax.experimental import pallas as pl
from jax.experimental.pallas import tpu as pltpu
from jax.sharding import PartitionSpec as P

spin_sign = (1.0, 1.0, -1.0, -1.0)
MESH = pl.DeviceIdType.MESH
NT = (((1,), (1,)), ((), ()))


def dot_nt(a, b):
    return lax.dot_general(a, b, NT, preferred_element_type=jnp.float32)


def kernel(
    sizes,
    tiles_hbm, elem_hbm, order_hbm, column_hbm,
    out_ref,
    tiles, elem, order, column,
    near, coef, left, mirror, forward, partial, result, total,
    gone, tile_recv, coef_recv, share_recv, result_recv, above,
):
    src_count, col_count, half_count = sizes
    blocks = col_count * half_count
    half = blocks // 2
    block_cols, components = tiles.shape[2], tiles.shape[3]
    eigen = elem.shape[-1]
    spins = components // eigen
    piece = eigen // blocks
    last = src_count - 1
    p = lax.axis_index("src")
    b = lax.axis_index("col") * half_count + lax.axis_index("half")
    offsets = [2 * j if j < half else 2 * (j - half) + 1 for j in range(blocks)]
    each = functools.partial(pl.loop, unroll=src_count <= 8)

    def device(slot, block):
        return {
            "src": slot,
            "col": lax.div(block, half_count),
            "half": lax.rem(block, half_count),
        }

    def signal(sem, slot, block):
        pl.semaphore_signal(sem, inc=1, device_id=device(slot, block), device_id_type=MESH)

    def send(src, dst, recv_sem, slot, block):
        pltpu.make_async_remote_copy(
            src_ref=src, dst_ref=dst, send_sem=gone, recv_sem=recv_sem,
            device_id=device(slot, block), device_id_type=MESH,
        ).start()

    def wait_bytes(ref, sem):
        pltpu.make_async_copy(ref, ref, sem).wait()

    def shifted(block, offset):
        return lax.rem(block + offset + blocks, blocks)

    def spin_of(block):
        if isinstance(block, int):
            return block * block_cols // eigen
        return lax.div(block * block_cols, eigen)

    def sign_of(block):
        return jnp.where(spin_of(block) < 2, spin_sign[0], spin_sign[2]).astype(jnp.float32)

    def rows_of(block):
        if isinstance(block, int):
            return pl.ds(block * block_cols % eigen, block_cols)
        return pl.ds(pl.multiple_of(lax.rem(block * block_cols, eigen), block_cols), block_cols)

    def upward(low, high):
        whole = jnp.where(jnp.logical_or(lax.rem(high, 2) == 0, high - low == 1), blocks, 0)
        return jnp.where(high == 1, 1, whole)

    def count(source, target):
        n = upward(jnp.minimum(source, target), jnp.maximum(source, target))
        return jnp.where(source < target, n, blocks - n)

    def goes(source, target, j):
        n = upward(jnp.minimum(source, target), jnp.maximum(source, target))
        return jnp.where(source < target, j < n, j >= n)

    barrier = pltpu.get_barrier_semaphore()

    for k in range(1, blocks):
        signal(barrier, p, shifted(b, k))

    @each(0, src_count)
    def _(slot):
        @pl.when(slot > p)
        def _():
            for k in range(blocks):
                signal(barrier, slot, k)

    loads = [
        pltpu.make_async_copy(elem_hbm.at[0, 0], elem, coef_recv.at[p]),
        pltpu.make_async_copy(column_hbm, column, share_recv.at[p]),
        pltpu.make_async_copy(order_hbm, order, tile_recv.at[p, 1]),
        pltpu.make_async_copy(tiles_hbm.at[0], tiles, tile_recv.at[p, 2]),
    ]
    for load in loads:
        load.start()

    pl.semaphore_wait(barrier, blocks - 1 + p * blocks)

    @each(0, src_count)
    def _(slot):
        @pl.when(slot < p)
        def _():
            signal(above.at[p], slot, b)

    loads[0].wait()
    loads[1].wait()
    pick = (
        lax.broadcasted_iota(jnp.int32, (eigen, eigen), 0) == column[...]
    ).astype(jnp.float32).T.astype(jnp.bfloat16)
    both = jnp.concatenate([elem[0], elem[1]], axis=1)
    picked = jnp.dot(pick, both, preferred_element_type=jnp.float32).astype(jnp.bfloat16)
    coef[p, 0] = picked[:, :eigen]
    coef[p, 1] = picked[:, eigen:]

    loads[2].wait()
    loads[3].wait()

    def sort(slot):
        for spin in range(spins):
            near[slot, spin] = tiles[order[slot], :, :, spin * eigen : (spin + 1) * eigen]

    my_piece = pl.ds(pl.multiple_of(b * piece, piece), piece)

    def send_coef(slot):
        @pl.when(count(p, slot) > 0)
        def _():
            send(
                coef.at[p, :, my_piece, :], coef.at[p, :, my_piece, :],
                coef_recv.at[p], slot, b,
            )

    groups = [(0, 1), (1, half), (half, blocks)]

    def group_of(j):
        return [start <= j < stop for start, stop in groups].index(True)

    def offset_of(j):
        return jnp.where(lax.rem(b, 2) == 0, offsets[j], offsets[j ^ 1])

    def send_unit(slot, j):
        @pl.when(goes(p, slot, j))
        def _():
            block = jnp.where(p < slot, shifted(b, offset_of(j)), shifted(b, -offset_of(j)))
            send(
                near.at[slot, spin_of(block)], mirror.at[p, b],
                tile_recv.at[p, group_of(j)], slot, block,
            )

    def send_units(slot, start, stop):
        for j in range(start, stop):
            send_unit(slot, j)

    @each(0, src_count)
    def _(slot):
        @pl.when(slot < p)
        def _():
            send_coef(slot)

    @each(0, src_count)
    def _(slot):
        @pl.when(slot < p)
        def _():
            sort(slot)
            send_units(slot, 0, blocks)

    @each(0, src_count)
    def _(slot):
        @pl.when(slot >= p)
        def _():
            sort(slot)

    @pl.when(p < last)
    def _():
        pl.semaphore_wait(above.at[p + 1], 1)
        send_coef(p + 1)
        send_units(p + 1, 0, 1)

    @each(0, src_count)
    def _(slot):
        @pl.when(slot > p + 1)
        def _():
            pl.semaphore_wait(above.at[slot], 1)
            send_coef(slot)
            send_units(slot, 0, blocks)

    @pl.when(p < last)
    def _():
        send_units(p + 1, 1, blocks)

    def others(act):
        @each(0, src_count)
        def _(slot):
            @pl.when(slot != p)
            def _():
                act(slot)

    def share_coef(slot):
        @pl.when(count(slot, p) > 0)
        def _():
            wait_bytes(coef.at[slot, :, pl.ds(0, piece), :], coef_recv.at[slot])
            for k in range(1, blocks):
                send(
                    coef.at[slot, :, my_piece, :], coef.at[slot, :, my_piece, :],
                    share_recv.at[slot], p, shifted(b, k),
                )

    def diag_source(k):
        return b >= half if k == half else b >= 0

    def diag_target(k):
        return b < half if k == half else b >= 0

    for k in range(1, half + 1):
        @pl.when(diag_source(k))
        def _():
            block = shifted(b, -k)
            send(
                near.at[p, spin_of(block)], mirror.at[p, b],
                tile_recv.at[p, 0], p, block,
            )

    own_real, own_imag = coef[p, 0, rows_of(b), :], coef[p, 1, rows_of(b), :]
    left[:block_cols, :eigen] = own_real
    left[:block_cols, eigen:] = -own_imag
    left[block_cols:, :eigen] = own_imag
    left[block_cols:, eigen:] = own_real

    def make_forward(slot, block):
        far_real, far_imag = coef[slot, 0, rows_of(block), :], coef[slot, 1, rows_of(block), :]
        mine = jnp.concatenate([near[slot, spin_of(block), 0], near[slot, spin_of(block), 1]], axis=1)
        real = jnp.concatenate([far_real, -far_imag], axis=1)
        imag = jnp.concatenate([far_imag, far_real], axis=1)
        product = dot_nt(jnp.concatenate([real, imag], axis=0), mine).astype(jnp.bfloat16)
        forward[slot, block, 0] = product[:block_cols]
        forward[slot, block, 1] = product[block_cols:]

    def fold(value):
        return jnp.sum(value.reshape(block_cols // 8, 8, block_cols), axis=0)

    def multiply(slot, block, away, weight, first):
        backward = dot_nt(jnp.concatenate([away[0], away[1]], axis=1), left[...])
        backward = backward.astype(jnp.bfloat16).astype(jnp.float32)
        br, bi = backward[:, :block_cols], backward[:, block_cols:]
        fr = forward[slot, block, 0].astype(jnp.float32)
        fi = forward[slot, block, 1].astype(jnp.float32)
        scale = weight * sign_of(block) * sign_of(b)
        real = scale * fold(fr * br - fi * bi)
        imag = scale * fold(fr * bi + fi * br)
        packed = jnp.concatenate([real[:4] + real[4:], imag[:4] + imag[4:]], axis=0)
        if first:
            partial[slot] = packed
        else:
            partial[slot] += packed

    def share_result(slot):
        result[slot, b] = partial[slot]
        for k in range(1, blocks):
            block = shifted(b, k)
            send(
                result.at[slot, b], result.at[slot, b],
                result_recv.at[slot], p, block,
            )

    def send_result(slot):
        for k in range(blocks):
            block = shifted(b, k)
            send(
                result.at[slot, b], result.at[p, blocks + b],
                result_recv.at[p], slot, block,
            )

    make_forward(p, b)
    multiply(p, b, near[p, spin_of(b)], 1.0, True)
    for k in range(1, half + 1):
        @pl.when(diag_target(k))
        def _():
            make_forward(p, shifted(b, k))

    @each(0, src_count)
    def _(step):
        @pl.when(step < p)
        def _():
            share_coef(p - 1 - step)

    @each(0, src_count)
    def _(slot):
        @pl.when(slot > p)
        def _():
            share_coef(slot)


    def take_diagonal():
        for n in (half - 1, half):
            @pl.when(diag_target(half) == (n == half))
            def _():
                wait_bytes(mirror.at[p, pl.ds(0, n)], tile_recv.at[p, 0])

        for k in range(1, half + 1):
            @pl.when(diag_target(k))
            def _():
                block = shifted(b, k)
                multiply(p, block, mirror[p, block], 2.0, False)
        share_result(p)

    def source_block(slot, j):
        return jnp.where(slot < p, shifted(b, -offset_of(j)), shifted(b, offset_of(j)))

    def prepare(slot):
        @pl.when(count(slot, p) > 0)
        def _():
            wait_bytes(coef.at[slot, :, pl.ds(0, eigen - piece), :], share_recv.at[slot])
            partial[slot] = jnp.zeros(partial.shape[1:], jnp.float32)
            for block in range(blocks):
                make_forward(slot, block)

    def take_units(slot, start, stop):
        @pl.when(goes(slot, p, start))
        def _():
            wait_bytes(mirror.at[slot, pl.ds(0, stop - start)], tile_recv.at[slot, group_of(start)])
            for j in range(start, stop):
                block = source_block(slot, j)
                multiply(slot, block, mirror[slot, block], 1.0, False)

    def finish(slot):
        @pl.when(count(slot, p) > 0)
        def _():
            share_result(slot)
            send_result(slot)

    def take_all(slot):
        for start, stop in groups:
            take_units(slot, start, stop)
        finish(slot)

    @each(0, src_count)
    def _(slot):
        @pl.when(slot != p)
        def _():
            prepare(slot)
            take_all(slot)

        @pl.when(slot == jnp.where(p == 0, 1, 0))
        def _():
            take_diagonal()

    for k in range(1, half + 1):
        @pl.when(diag_source(k))
        def _():
            wait_bytes(mirror.at[p, 0], gone)

    @each(0, src_count)
    def _(slot):
        @pl.when(slot != p)
        def _():
            sent, received = count(p, slot), count(slot, p)

            @pl.when(sent > 0)
            def _():
                wait_bytes(coef.at[slot, :, pl.ds(0, piece), :], gone)

            for n in range(1, blocks + 1):
                @pl.when(sent == n)
                def _():
                    wait_bytes(mirror.at[slot, pl.ds(0, n)], gone)

            @pl.when(received > 0)
            def _():
                wait_bytes(coef.at[slot, :, pl.ds(0, eigen - piece), :], gone)

    @each(0, src_count)
    def _(slot):
        here = jnp.logical_or(slot == p, count(slot, p) > 0)
        there = jnp.logical_and(slot != p, count(p, slot) > 0)
        expected = jnp.where(here, blocks - 1, 0) + jnp.where(there, blocks, 0)
        for n in (blocks - 1, blocks, 2 * blocks - 1):
            @pl.when(expected == n)
            def _():
                wait_bytes(result.at[slot, pl.ds(0, n)], result_recv.at[slot])

    @each(0, src_count)
    def _(slot):
        total[slot] = jnp.zeros(total.shape[1:], jnp.float32)

        @pl.when(jnp.logical_or(slot == p, count(slot, p) > 0))
        def _():
            total[slot] += jnp.sum(result[slot, :blocks], axis=0)

        @pl.when(jnp.logical_and(slot != p, count(p, slot) > 0))
        def _():
            total[slot] += jnp.sum(result[slot, blocks:], axis=0)

    rows = jnp.concatenate(
        [
            jnp.sum(total[slot, 4 * part : 4 * part + 4], axis=0, keepdims=True)
            for part in (0, 1)
            for slot in range(src_count)
        ],
        axis=0,
    )
    sums = jnp.sum(rows, axis=1, keepdims=True)
    lane = lax.broadcasted_iota(jnp.int32, (src_count, src_count), 1)
    row = lax.broadcasted_iota(jnp.int32, (src_count, src_count), 0)
    for part in (0, 1):
        picked = jnp.where(lane == row, sums[part * src_count : (part + 1) * src_count], 0.0)
        out_ref[0, part, 0] = jnp.sum(picked, axis=0, keepdims=True)

    wait_bytes(result.at[p, pl.ds(0, blocks - 1)], gone)

    @each(0, src_count)
    def _(slot):
        @pl.when(jnp.logical_and(slot != p, count(slot, p) > 0))
        def _():
            wait_bytes(result.at[slot, pl.ds(0, blocks)], gone)
            wait_bytes(result.at[slot, pl.ds(0, blocks - 1)], gone)


def on_device(sizes, perambulator, elemental, source_order, column_order):
    operators = elemental.shape[0]
    eigen = elemental.shape[-1]
    _, slots, _, block_cols, components = perambulator.shape
    src_count, col_count, half_count = sizes
    blocks = col_count * half_count
    spins = components // eigen
    sem = pltpu.SemaphoreType.DMA
    flag = pltpu.SemaphoreType.REGULAR
    return pl.pallas_call(
        functools.partial(kernel, sizes),
        out_shape=pltpu.VMEM((1, 2, operators, operators, slots), jnp.float32),
        in_specs=[pl.BlockSpec(memory_space=pl.ANY)] * 4,
        out_specs=pl.BlockSpec(memory_space=pltpu.VMEM),
        scratch_shapes=[
            pltpu.VMEM((slots, 2, block_cols, components), jnp.bfloat16),
            pltpu.VMEM((2, eigen, eigen), jnp.bfloat16),
            pltpu.SMEM((slots,), jnp.int32),
            pltpu.VMEM((1, eigen), jnp.int32),
            pltpu.VMEM((slots, spins, 2, block_cols, eigen), jnp.bfloat16),
            pltpu.VMEM((slots, 2, eigen, eigen), jnp.bfloat16),
            pltpu.VMEM((2 * block_cols, 2 * eigen), jnp.bfloat16),
            pltpu.VMEM((slots, blocks, 2, block_cols, eigen), jnp.bfloat16),
            pltpu.VMEM((slots, blocks, 2, block_cols, block_cols), jnp.bfloat16),
            pltpu.VMEM((slots, 8, block_cols), jnp.float32),
            pltpu.VMEM((slots, 2 * blocks, 8, block_cols), jnp.float32),
            pltpu.VMEM((slots, 8, block_cols), jnp.float32),
            sem,
            sem((slots, 3)),
            sem((slots,)),
            sem((slots,)),
            sem((slots,)),
            flag((slots,)),
        ],
        compiler_params=pltpu.CompilerParams(collective_id=0, has_side_effects=True),
    )(perambulator, elemental, source_order, column_order)


def solution(mesh):
    sizes = (mesh.shape["src"], mesh.shape["col"], mesh.shape["half"])
    return jax.shard_map(
        functools.partial(on_device, sizes),
        mesh=mesh,
        in_specs=(
            P(("cfg", "src"), None, None, ("col", "half"), None),
            P(None, ("cfg", "src"), None, None, None),
            P("cfg"),
            P(("cfg", "src"), None),
        ),
        out_specs=P(("cfg", "src"), None, None, None, None),
        check_vma=False,
    )
```

```python
import functools

import jax
import jax.numpy as jnp
from jax import lax
from jax.experimental import pallas as pl
from jax.experimental.pallas import tpu as pltpu
from jax.sharding import PartitionSpec as P

spin_sign = (1.0, 1.0, -1.0, -1.0)
MESH = pl.DeviceIdType.MESH
NT = (((1,), (1,)), ((), ()))


def dot_nt(a, b):
    return lax.dot_general(a, b, NT, preferred_element_type=jnp.float32)


def kernel(
    sizes,
    tiles_hbm, elem_hbm, order_hbm, column_hbm,
    out_ref,
    tiles, elem, order, column,
    near, coef, left, mirror, forward, partial, result, total,
    gone, tile_recv, coef_recv, share_recv, result_recv, above,
):
    src_count, col_count, half_count = sizes
    blocks = col_count * half_count
    half = blocks // 2
    block_cols, components = tiles.shape[2], tiles.shape[3]
    eigen = elem.shape[-1]
    spins = components // eigen
    piece = eigen // blocks
    last = src_count - 1
    p = lax.axis_index("src")
    b = lax.axis_index("col") * half_count + lax.axis_index("half")
    offsets = [2 * j if j < half else 2 * (j - half) + 1 for j in range(blocks)]
    each = functools.partial(pl.loop, unroll=src_count <= 8)

    def device(slot, block):
        return {
            "src": slot,
            "col": lax.div(block, half_count),
            "half": lax.rem(block, half_count),
        }

    def signal(sem, slot, block):
        pl.semaphore_signal(sem, inc=1, device_id=device(slot, block), device_id_type=MESH)

    def send(src, dst, recv_sem, slot, block):
        pltpu.make_async_remote_copy(
            src_ref=src, dst_ref=dst, send_sem=gone, recv_sem=recv_sem,
            device_id=device(slot, block), device_id_type=MESH,
        ).start()

    def wait_bytes(ref, sem):
        pltpu.make_async_copy(ref, ref, sem).wait()

    def shifted(block, offset):
        return lax.rem(block + offset + blocks, blocks)

    def spin_of(block):
        if isinstance(block, int):
            return block * block_cols // eigen
        return lax.div(block * block_cols, eigen)

    def sign_of(block):
        return jnp.where(spin_of(block) < 2, spin_sign[0], spin_sign[2]).astype(jnp.float32)

    def rows_of(block):
        if isinstance(block, int):
            return pl.ds(block * block_cols % eigen, block_cols)
        return pl.ds(pl.multiple_of(lax.rem(block * block_cols, eigen), block_cols), block_cols)

    def upward(low, high):
        whole = jnp.where(jnp.logical_or(lax.rem(high, 2) == 0, high - low == 1), blocks, 0)
        return jnp.where(high == 1, half, whole)

    def count(source, target):
        n = upward(jnp.minimum(source, target), jnp.maximum(source, target))
        return jnp.where(source < target, n, blocks - n)

    def goes(source, target, j):
        n = upward(jnp.minimum(source, target), jnp.maximum(source, target))
        return jnp.where(source < target, j < n, j >= n)

    barrier = pltpu.get_barrier_semaphore()

    for k in range(1, blocks):
        signal(barrier, p, shifted(b, k))

    @each(0, src_count)
    def _(slot):
        @pl.when(slot > p)
        def _():
            for k in range(blocks):
                signal(barrier, slot, k)

    loads = [
        pltpu.make_async_copy(elem_hbm.at[0, 0], elem, coef_recv.at[p]),
        pltpu.make_async_copy(column_hbm, column, share_recv.at[p]),
        pltpu.make_async_copy(order_hbm, order, tile_recv.at[p, 2]),
        pltpu.make_async_copy(tiles_hbm.at[0], tiles, tile_recv.at[p, 1]),
    ]
    for load in loads:
        load.start()

    first_column = b < half_count

    def greet():
        pl.semaphore_wait(barrier, blocks - 1 + p * blocks)

        @each(0, src_count)
        def _(slot):
            @pl.when(slot < p)
            def _():
                signal(above.at[p], slot, b)

    pl.when(jnp.logical_not(first_column))(greet)

    loads[0].wait()
    loads[1].wait()
    pick = (
        lax.broadcasted_iota(jnp.int32, (eigen, eigen), 0) == column[...]
    ).astype(jnp.float32).T.astype(jnp.bfloat16)
    both = jnp.concatenate([elem[0], elem[1]], axis=1)
    picked = jnp.dot(pick, both, preferred_element_type=jnp.float32).astype(jnp.bfloat16)
    coef[p, 0] = picked[:, :eigen]
    coef[p, 1] = picked[:, eigen:]

    loads[2].wait()
    loads[3].wait()
    pl.when(first_column)(greet)

    def sort(slot):
        for spin in range(spins):
            near[slot, spin] = tiles[order[slot], :, :, spin * eigen : (spin + 1) * eigen]

    my_piece = pl.ds(pl.multiple_of(b * piece, piece), piece)

    def send_coef(slot):
        @pl.when(count(p, slot) > 0)
        def _():
            send(
                coef.at[p, :, my_piece, :], coef.at[p, :, my_piece, :],
                coef_recv.at[p], slot, b,
            )

    groups = [(0, half), (half, blocks - 1), (blocks - 1, blocks)]

    def group_of(j):
        return [start <= j < stop for start, stop in groups].index(True)

    def offset_of(j):
        return offsets[j]

    def send_unit(slot, j):
        @pl.when(goes(p, slot, j))
        def _():
            block = jnp.where(p < slot, shifted(b, offset_of(j)), shifted(b, -offset_of(j)))
            send(
                near.at[slot, spin_of(block)], mirror.at[p, b],
                tile_recv.at[p, group_of(j)], slot, block,
            )

    def send_units(slot, start, stop):
        for j in range(start, stop):
            send_unit(slot, j)

    @each(0, src_count)
    def _(slot):
        @pl.when(slot < p)
        def _():
            send_coef(slot)

    @each(0, src_count)
    def _(slot):
        @pl.when(slot < p)
        def _():
            sort(slot)
            send_units(slot, 0, blocks)

    @each(0, src_count)
    def _(slot):
        @pl.when(slot >= p)
        def _():
            sort(slot)

    @pl.when(p < last)
    def _():
        pl.semaphore_wait(above.at[p + 1], 1)
        send_coef(p + 1)
        send_units(p + 1, 0, 1)

        @pl.when(p == 0)
        def _():
            send_units(p + 1, 1, blocks)


    @each(0, src_count)
    def _(slot):
        @pl.when(slot > p + 1)
        def _():
            pl.semaphore_wait(above.at[slot], 1)
            send_coef(slot)
            send_units(slot, 0, blocks)

    @pl.when(jnp.logical_and(p > 0, p < last))
    def _():
        send_units(p + 1, 1, blocks)

    def others(act):
        @each(0, src_count)
        def _(slot):
            @pl.when(slot != p)
            def _():
                act(slot)

    def share_coef(slot):
        @pl.when(count(slot, p) > 0)
        def _():
            wait_bytes(coef.at[slot, :, pl.ds(0, piece), :], coef_recv.at[slot])
            for k in range(1, blocks):
                send(
                    coef.at[slot, :, my_piece, :], coef.at[slot, :, my_piece, :],
                    share_recv.at[slot], p, shifted(b, k),
                )

    def diag_source(k):
        return b >= half if k == half else b >= 0

    def diag_target(k):
        return b < half if k == half else b >= 0

    for k in range(1, half + 1):
        @pl.when(diag_source(k))
        def _():
            block = shifted(b, -k)
            send(
                near.at[p, spin_of(block)], mirror.at[p, b],
                tile_recv.at[p, 0], p, block,
            )

    own_real, own_imag = coef[p, 0, rows_of(b), :], coef[p, 1, rows_of(b), :]
    left[:block_cols, :eigen] = own_real
    left[:block_cols, eigen:] = -own_imag
    left[block_cols:, :eigen] = own_imag
    left[block_cols:, eigen:] = own_real

    def make_forward(slot, block):
        far_real, far_imag = coef[slot, 0, rows_of(block), :], coef[slot, 1, rows_of(block), :]
        mine = jnp.concatenate([near[slot, spin_of(block), 0], near[slot, spin_of(block), 1]], axis=1)
        real = jnp.concatenate([far_real, -far_imag], axis=1)
        imag = jnp.concatenate([far_imag, far_real], axis=1)
        product = dot_nt(jnp.concatenate([real, imag], axis=0), mine).astype(jnp.bfloat16)
        forward[slot, block, 0] = product[:block_cols]
        forward[slot, block, 1] = product[block_cols:]

    def fold(value):
        return jnp.sum(value.reshape(block_cols // 8, 8, block_cols), axis=0)

    def multiply(slot, block, away, weight, first):
        backward = dot_nt(jnp.concatenate([away[0], away[1]], axis=1), left[...])
        backward = backward.astype(jnp.bfloat16).astype(jnp.float32)
        br, bi = backward[:, :block_cols], backward[:, block_cols:]
        fr = forward[slot, block, 0].astype(jnp.float32)
        fi = forward[slot, block, 1].astype(jnp.float32)
        scale = weight * sign_of(block) * sign_of(b)
        real = scale * fold(fr * br - fi * bi)
        imag = scale * fold(fr * bi + fi * br)
        packed = jnp.concatenate([real[:4] + real[4:], imag[:4] + imag[4:]], axis=0)
        if first:
            partial[slot] = packed
        else:
            partial[slot] += packed

    def share_result(slot):
        result[slot, b] = partial[slot]
        for k in range(1, blocks):
            block = shifted(b, k)
            send(
                result.at[slot, b], result.at[slot, b],
                result_recv.at[slot], p, block,
            )

    def send_result(slot):
        for k in range(blocks):
            block = shifted(b, k)
            send(
                result.at[slot, b], result.at[p, blocks + b],
                result_recv.at[p], slot, block,
            )

    make_forward(p, b)
    multiply(p, b, near[p, spin_of(b)], 1.0, True)
    for k in range(1, half + 1):
        @pl.when(diag_target(k))
        def _():
            make_forward(p, shifted(b, k))

    @each(0, src_count)
    def _(step):
        @pl.when(step < p)
        def _():
            share_coef(p - 1 - step)

    @each(0, src_count)
    def _(slot):
        @pl.when(slot > p)
        def _():
            share_coef(slot)


    def take_diagonal():
        for n in (half - 1, half):
            @pl.when(diag_target(half) == (n == half))
            def _():
                wait_bytes(mirror.at[p, pl.ds(0, n)], tile_recv.at[p, 0])

        for k in range(1, half + 1):
            @pl.when(diag_target(k))
            def _():
                block = shifted(b, k)
                multiply(p, block, mirror[p, block], 2.0, False)
        share_result(p)

    def source_block(slot, j):
        return jnp.where(slot < p, shifted(b, -offset_of(j)), shifted(b, offset_of(j)))

    def prepare(slot):
        @pl.when(count(slot, p) > 0)
        def _():
            wait_bytes(coef.at[slot, :, pl.ds(0, eigen - piece), :], share_recv.at[slot])
            partial[slot] = jnp.zeros(partial.shape[1:], jnp.float32)
            for block in range(blocks):
                make_forward(slot, block)

    def take_units(slot, start, stop):
        @pl.when(goes(slot, p, start))
        def _():
            wait_bytes(mirror.at[slot, pl.ds(0, stop - start)], tile_recv.at[slot, group_of(start)])
            for j in range(start, stop):
                block = source_block(slot, j)
                multiply(slot, block, mirror[slot, block], 1.0, False)

    def finish(slot):
        @pl.when(count(slot, p) > 0)
        def _():
            share_result(slot)
            send_result(slot)

    def take_all(slot):
        for start, stop in groups:
            take_units(slot, start, stop)
        finish(slot)

    @each(0, src_count)
    def _(slot):
        @pl.when(slot != p)
        def _():
            prepare(slot)
            take_all(slot)

        @pl.when(slot == jnp.where(p == 0, 1, 0))
        def _():
            take_diagonal()

    for k in range(1, half + 1):
        @pl.when(diag_source(k))
        def _():
            wait_bytes(mirror.at[p, 0], gone)

    @each(0, src_count)
    def _(slot):
        @pl.when(slot != p)
        def _():
            sent, received = count(p, slot), count(slot, p)

            @pl.when(sent > 0)
            def _():
                wait_bytes(coef.at[slot, :, pl.ds(0, piece), :], gone)

            for n in range(1, blocks + 1):
                @pl.when(sent == n)
                def _():
                    wait_bytes(mirror.at[slot, pl.ds(0, n)], gone)

            @pl.when(received > 0)
            def _():
                wait_bytes(coef.at[slot, :, pl.ds(0, eigen - piece), :], gone)

    @each(0, src_count)
    def _(slot):
        here = jnp.logical_or(slot == p, count(slot, p) > 0)
        there = jnp.logical_and(slot != p, count(p, slot) > 0)
        expected = jnp.where(here, blocks - 1, 0) + jnp.where(there, blocks, 0)
        for n in (blocks - 1, blocks, 2 * blocks - 1):
            @pl.when(expected == n)
            def _():
                wait_bytes(result.at[slot, pl.ds(0, n)], result_recv.at[slot])

        total[slot] = jnp.zeros(total.shape[1:], jnp.float32)

        @pl.when(jnp.logical_or(slot == p, count(slot, p) > 0))
        def _():
            total[slot] += jnp.sum(result[slot, :blocks], axis=0)

        @pl.when(jnp.logical_and(slot != p, count(p, slot) > 0))
        def _():
            total[slot] += jnp.sum(result[slot, blocks:], axis=0)

    rows = jnp.concatenate(
        [
            jnp.sum(total[slot, 4 * part : 4 * part + 4], axis=0, keepdims=True)
            for part in (0, 1)
            for slot in range(src_count)
        ],
        axis=0,
    )
    sums = jnp.sum(rows, axis=1, keepdims=True)
    lane = lax.broadcasted_iota(jnp.int32, (src_count, src_count), 1)
    row = lax.broadcasted_iota(jnp.int32, (src_count, src_count), 0)
    for part in (0, 1):
        picked = jnp.where(lane == row, sums[part * src_count : (part + 1) * src_count], 0.0)
        out_ref[0, part, 0] = jnp.sum(picked, axis=0, keepdims=True)

    wait_bytes(result.at[p, pl.ds(0, blocks - 1)], gone)

    @each(0, src_count)
    def _(slot):
        @pl.when(jnp.logical_and(slot != p, count(slot, p) > 0))
        def _():
            wait_bytes(result.at[slot, pl.ds(0, blocks)], gone)
            wait_bytes(result.at[slot, pl.ds(0, blocks - 1)], gone)


def on_device(sizes, perambulator, elemental, source_order, column_order):
    operators = elemental.shape[0]
    eigen = elemental.shape[-1]
    _, slots, _, block_cols, components = perambulator.shape
    src_count, col_count, half_count = sizes
    blocks = col_count * half_count
    spins = components // eigen
    sem = pltpu.SemaphoreType.DMA
    flag = pltpu.SemaphoreType.REGULAR
    return pl.pallas_call(
        functools.partial(kernel, sizes),
        out_shape=pltpu.VMEM((1, 2, operators, operators, slots), jnp.float32),
        in_specs=[pl.BlockSpec(memory_space=pl.ANY)] * 4,
        out_specs=pl.BlockSpec(memory_space=pltpu.VMEM),
        scratch_shapes=[
            pltpu.VMEM((slots, 2, block_cols, components), jnp.bfloat16),
            pltpu.VMEM((2, eigen, eigen), jnp.bfloat16),
            pltpu.SMEM((slots,), jnp.int32),
            pltpu.VMEM((1, eigen), jnp.int32),
            pltpu.VMEM((slots, spins, 2, block_cols, eigen), jnp.bfloat16),
            pltpu.VMEM((slots, 2, eigen, eigen), jnp.bfloat16),
            pltpu.VMEM((2 * block_cols, 2 * eigen), jnp.bfloat16),
            pltpu.VMEM((slots, blocks, 2, block_cols, eigen), jnp.bfloat16),
            pltpu.VMEM((slots, blocks, 2, block_cols, block_cols), jnp.bfloat16),
            pltpu.VMEM((slots, 8, block_cols), jnp.float32),
            pltpu.VMEM((slots, 2 * blocks, 8, block_cols), jnp.float32),
            pltpu.VMEM((slots, 8, block_cols), jnp.float32),
            sem,
            sem((slots, 3)),
            sem((slots,)),
            sem((slots,)),
            sem((slots,)),
            flag((slots,)),
        ],
        compiler_params=pltpu.CompilerParams(collective_id=0, has_side_effects=True),
    )(perambulator, elemental, source_order, column_order)


def solution(mesh):
    sizes = (mesh.shape["src"], mesh.shape["col"], mesh.shape["half"])
    return jax.shard_map(
        functools.partial(on_device, sizes),
        mesh=mesh,
        in_specs=(
            P(("cfg", "src"), None, None, ("col", "half"), None),
            P(None, ("cfg", "src"), None, None, None),
            P("cfg"),
            P(("cfg", "src"), None),
        ),
        out_specs=P(("cfg", "src"), None, None, None, None),
        check_vma=False,
    )
```

```python
import functools

import jax
import jax.numpy as jnp
from jax import lax
from jax.experimental import pallas as pl
from jax.experimental.pallas import tpu as pltpu
from jax.sharding import PartitionSpec as P

spin_sign = (1.0, 1.0, -1.0, -1.0)
MESH = pl.DeviceIdType.MESH
NT = (((1,), (1,)), ((), ()))


def dot_nt(a, b):
    return lax.dot_general(a, b, NT, preferred_element_type=jnp.float32)


def kernel(
    sizes,
    tiles_hbm, elem_hbm, order_hbm, column_hbm,
    out_ref,
    tiles, elem, order, column,
    near, coef, left, mirror, forward, partial, result, total,
    gone, tile_recv, coef_recv, share_recv, result_recv, above,
):
    src_count, col_count, half_count = sizes
    blocks = col_count * half_count
    half = blocks // 2
    block_cols, components = tiles.shape[2], tiles.shape[3]
    eigen = elem.shape[-1]
    spins = components // eigen
    piece = eigen // blocks
    last = src_count - 1
    p = lax.axis_index("src")
    b = lax.axis_index("col") * half_count + lax.axis_index("half")
    offsets = [2 * j if j < half else 2 * (j - half) + 1 for j in range(blocks)]
    each = functools.partial(pl.loop, unroll=src_count <= 8)

    def device(slot, block):
        return {
            "src": slot,
            "col": lax.div(block, half_count),
            "half": lax.rem(block, half_count),
        }

    def signal(sem, slot, block):
        pl.semaphore_signal(sem, inc=1, device_id=device(slot, block), device_id_type=MESH)

    def send(src, dst, recv_sem, slot, block):
        pltpu.make_async_remote_copy(
            src_ref=src, dst_ref=dst, send_sem=gone, recv_sem=recv_sem,
            device_id=device(slot, block), device_id_type=MESH,
        ).start()

    def wait_bytes(ref, sem):
        pltpu.make_async_copy(ref, ref, sem).wait()

    def shifted(block, offset):
        return lax.rem(block + offset + blocks, blocks)

    def spin_of(block):
        if isinstance(block, int):
            return block * block_cols // eigen
        return lax.div(block * block_cols, eigen)

    def sign_of(block):
        return jnp.where(spin_of(block) < 2, spin_sign[0], spin_sign[2]).astype(jnp.float32)

    def rows_of(block):
        if isinstance(block, int):
            return pl.ds(block * block_cols % eigen, block_cols)
        return pl.ds(pl.multiple_of(lax.rem(block * block_cols, eigen), block_cols), block_cols)

    def upward(low, high):
        whole = jnp.where(jnp.logical_or(lax.rem(high, 2) == 0, high - low == 1), blocks, 0)
        return jnp.where(high == 1, half, whole)

    def count(source, target):
        n = upward(jnp.minimum(source, target), jnp.maximum(source, target))
        return jnp.where(source < target, n, blocks - n)

    def goes(source, target, j):
        n = upward(jnp.minimum(source, target), jnp.maximum(source, target))
        return jnp.where(source < target, j < n, j >= n)

    barrier = pltpu.get_barrier_semaphore()

    for k in range(1, blocks):
        signal(barrier, p, shifted(b, k))

    @each(0, src_count)
    def _(slot):
        @pl.when(slot > p)
        def _():
            for k in range(blocks):
                signal(barrier, slot, k)

    loads = [
        pltpu.make_async_copy(elem_hbm.at[0, 0], elem, coef_recv.at[p]),
        pltpu.make_async_copy(column_hbm, column, share_recv.at[p]),
        pltpu.make_async_copy(order_hbm, order, tile_recv.at[p, 2]),
        pltpu.make_async_copy(tiles_hbm.at[0], tiles, tile_recv.at[p, 1]),
    ]
    for load in loads:
        load.start()

    first_column = b < half_count

    def greet():
        pl.semaphore_wait(barrier, blocks - 1 + p * blocks)

        @each(0, src_count)
        def _(slot):
            @pl.when(slot < p)
            def _():
                signal(above.at[p], slot, b)

    pl.when(jnp.logical_not(first_column))(greet)

    loads[0].wait()
    loads[1].wait()
    pick = (
        lax.broadcasted_iota(jnp.int32, (eigen, eigen), 0) == column[...]
    ).astype(jnp.float32).T.astype(jnp.bfloat16)
    both = jnp.concatenate([elem[0], elem[1]], axis=1)
    picked = jnp.dot(pick, both, preferred_element_type=jnp.float32).astype(jnp.bfloat16)
    coef[p, 0] = picked[:, :eigen]
    coef[p, 1] = picked[:, eigen:]

    loads[2].wait()
    loads[3].wait()
    pl.when(first_column)(greet)

    def sort(slot):
        for spin in range(spins):
            near[slot, spin] = tiles[order[slot], :, :, spin * eigen : (spin + 1) * eigen]

    my_piece = pl.ds(pl.multiple_of(b * piece, piece), piece)

    def relayed(source, target):
        return (target == 0) & (source > 1) & (count(source, 1) > 0)

    def send_coef(slot):
        @pl.when((count(p, slot) > 0) & jnp.logical_not(relayed(p, slot)))
        def _():
            send(
                coef.at[p, :, my_piece, :], coef.at[p, :, my_piece, :],
                coef_recv.at[p], slot, b,
            )

    groups = [(0, half), (half, blocks - 1), (blocks - 1, blocks)]

    def group_of(j):
        return [start <= j < stop for start, stop in groups].index(True)

    def offset_of(j):
        return offsets[j]

    def send_unit(slot, j):
        @pl.when(goes(p, slot, j))
        def _():
            block = jnp.where(p < slot, shifted(b, offset_of(j)), shifted(b, -offset_of(j)))
            send(
                near.at[slot, spin_of(block)], mirror.at[p, b],
                tile_recv.at[p, group_of(j)], slot, block,
            )

    def send_units(slot, start, stop):
        for j in range(start, stop):
            send_unit(slot, j)

    @each(0, src_count)
    def _(slot):
        @pl.when(slot < p)
        def _():
            send_coef(slot)

    @each(0, src_count)
    def _(slot):
        @pl.when(slot < p)
        def _():
            sort(slot)
            send_units(slot, 0, half)

    @each(0, src_count)
    def _(slot):
        @pl.when(slot < p)
        def _():
            send_units(slot, half, blocks)

    @each(0, src_count)
    def _(slot):
        @pl.when(slot >= p)
        def _():
            sort(slot)

    @pl.when(p < last)
    def _():
        pl.semaphore_wait(above.at[p + 1], 1)
        send_coef(p + 1)
        send_units(p + 1, 0, 1)

        @pl.when(p == 0)
        def _():
            send_units(p + 1, 1, blocks)


    @each(0, src_count)
    def _(slot):
        @pl.when(slot > p + 1)
        def _():
            pl.semaphore_wait(above.at[slot], 1)
            send_coef(slot)
            send_units(slot, 0, blocks)

    @pl.when(jnp.logical_and(p > 0, p < last))
    def _():
        send_units(p + 1, 1, blocks)

    def others(act):
        @each(0, src_count)
        def _(slot):
            @pl.when(slot != p)
            def _():
                act(slot)

    def share_coef(slot):
        @pl.when(count(slot, p) > 0)
        def _():
            wait_bytes(coef.at[slot, :, pl.ds(0, piece), :], coef_recv.at[slot])

            @pl.when((p == 1) & (count(slot, 0) > 0) & relayed(slot, 0))
            def _():
                send(
                    coef.at[slot, :, my_piece, :], coef.at[slot, :, my_piece, :],
                    coef_recv.at[slot], 0, b,
                )

            for k in range(1, blocks):
                send(
                    coef.at[slot, :, my_piece, :], coef.at[slot, :, my_piece, :],
                    share_recv.at[slot], p, shifted(b, k),
                )

    def diag_source(k):
        return b >= half if k == half else b >= 0

    def diag_target(k):
        return b < half if k == half else b >= 0

    for k in range(1, half + 1):
        @pl.when(diag_source(k))
        def _():
            block = shifted(b, -k)
            send(
                near.at[p, spin_of(block)], mirror.at[p, b],
                tile_recv.at[p, 0], p, block,
            )

    own_real, own_imag = coef[p, 0, rows_of(b), :], coef[p, 1, rows_of(b), :]
    left[:block_cols, :eigen] = own_real
    left[:block_cols, eigen:] = -own_imag
    left[block_cols:, :eigen] = own_imag
    left[block_cols:, eigen:] = own_real

    def make_forward(slot, block):
        far_real, far_imag = coef[slot, 0, rows_of(block), :], coef[slot, 1, rows_of(block), :]
        mine = jnp.concatenate([near[slot, spin_of(block), 0], near[slot, spin_of(block), 1]], axis=1)
        real = jnp.concatenate([far_real, -far_imag], axis=1)
        imag = jnp.concatenate([far_imag, far_real], axis=1)
        product = dot_nt(jnp.concatenate([real, imag], axis=0), mine).astype(jnp.bfloat16)
        forward[slot, block, 0] = product[:block_cols]
        forward[slot, block, 1] = product[block_cols:]

    def fold(value):
        return jnp.sum(value.reshape(block_cols // 8, 8, block_cols), axis=0)

    def multiply(slot, block, away, weight, first):
        backward = dot_nt(jnp.concatenate([away[0], away[1]], axis=1), left[...])
        backward = backward.astype(jnp.bfloat16).astype(jnp.float32)
        br, bi = backward[:, :block_cols], backward[:, block_cols:]
        fr = forward[slot, block, 0].astype(jnp.float32)
        fi = forward[slot, block, 1].astype(jnp.float32)
        scale = weight * sign_of(block) * sign_of(b)
        real = scale * fold(fr * br - fi * bi)
        imag = scale * fold(fr * bi + fi * br)
        packed = jnp.concatenate([real[:4] + real[4:], imag[:4] + imag[4:]], axis=0)
        if first:
            partial[slot] = packed
        else:
            partial[slot] += packed

    def by_column(j):
        return jnp.where(lax.rem(b, 2) == 0, j, j ^ 1)

    def share_result(slot):
        for j in range(blocks):
            block = by_column(j)

            @pl.when(block != b)
            def _():
                send(result.at[slot, b], result.at[slot, b], result_recv.at[slot], p, block)

    def send_result(slot):
        for j in range(blocks):
            send(
                result.at[slot, b], result.at[p, blocks + b],
                result_recv.at[p], slot, by_column(j),
            )

    make_forward(p, b)
    multiply(p, b, near[p, spin_of(b)], 1.0, True)
    for k in range(1, half + 1):
        @pl.when(diag_target(k))
        def _():
            make_forward(p, shifted(b, k))

    @each(0, src_count)
    def _(step):
        @pl.when(step < p)
        def _():
            share_coef(p - 1 - step)

    @each(0, src_count)
    def _(slot):
        @pl.when(slot > p)
        def _():
            share_coef(slot)


    def take_diagonal():
        for n in (half - 1, half):
            @pl.when(diag_target(half) == (n == half))
            def _():
                wait_bytes(mirror.at[p, pl.ds(0, n)], tile_recv.at[p, 0])

        for k in range(1, half + 1):
            @pl.when(diag_target(k))
            def _():
                block = shifted(b, k)
                multiply(p, block, mirror[p, block], 2.0, False)
        result[p, b] = partial[p]
        share_result(p)

    def source_block(slot, j):
        return jnp.where(slot < p, shifted(b, -offset_of(j)), shifted(b, offset_of(j)))

    def prepare(slot):
        @pl.when(count(slot, p) > 0)
        def _():
            wait_bytes(coef.at[slot, :, pl.ds(0, eigen - piece), :], share_recv.at[slot])
            partial[slot] = jnp.zeros(partial.shape[1:], jnp.float32)
            for block in range(blocks):
                make_forward(slot, block)

    def take_units(slot, start, stop):
        @pl.when(goes(slot, p, start))
        def _():
            wait_bytes(mirror.at[slot, pl.ds(0, stop - start)], tile_recv.at[slot, group_of(start)])
            for j in range(start, stop):
                block = source_block(slot, j)
                multiply(slot, block, mirror[slot, block], 1.0, False)

    def finish(slot):
        @pl.when(count(slot, p) > 0)
        def _():
            result[slot, b] = partial[slot]

            @pl.when(slot < p)
            def _():
                send_result(slot)

            share_result(slot)

            @pl.when(slot > p)
            def _():
                send_result(slot)

    def take_all(slot):
        for start, stop in groups:
            take_units(slot, start, stop)
        finish(slot)

    @each(0, src_count)
    def _(slot):
        @pl.when(slot != p)
        def _():
            prepare(slot)
            take_all(slot)

        @pl.when(slot == jnp.where(p == 0, 1, 0))
        def _():
            take_diagonal()

    for k in range(1, half + 1):
        @pl.when(diag_source(k))
        def _():
            wait_bytes(mirror.at[p, 0], gone)

    @each(0, src_count)
    def _(slot):
        @pl.when(slot != p)
        def _():
            sent, received = count(p, slot), count(slot, p)

            @pl.when((sent > 0) & jnp.logical_not(relayed(p, slot)))
            def _():
                wait_bytes(coef.at[slot, :, pl.ds(0, piece), :], gone)

            @pl.when((p == 1) & (received > 0) & (count(slot, 0) > 0) & relayed(slot, 0))
            def _():
                wait_bytes(coef.at[slot, :, pl.ds(0, piece), :], gone)

            for n in range(1, blocks + 1):
                @pl.when(sent == n)
                def _():
                    wait_bytes(mirror.at[slot, pl.ds(0, n)], gone)

            @pl.when(received > 0)
            def _():
                wait_bytes(coef.at[slot, :, pl.ds(0, eigen - piece), :], gone)

    @each(0, src_count)
    def _(slot):
        here = jnp.logical_or(slot == p, count(slot, p) > 0)
        there = jnp.logical_and(slot != p, count(p, slot) > 0)
        expected = jnp.where(here, blocks - 1, 0) + jnp.where(there, blocks, 0)
        for n in (blocks - 1, blocks, 2 * blocks - 1):
            @pl.when(expected == n)
            def _():
                wait_bytes(result.at[slot, pl.ds(0, n)], result_recv.at[slot])

        total[slot] = jnp.zeros(total.shape[1:], jnp.float32)

        @pl.when(jnp.logical_or(slot == p, count(slot, p) > 0))
        def _():
            total[slot] += jnp.sum(result[slot, :blocks], axis=0)

        @pl.when(jnp.logical_and(slot != p, count(p, slot) > 0))
        def _():
            total[slot] += jnp.sum(result[slot, blocks:], axis=0)

    rows = jnp.concatenate(
        [
            jnp.sum(total[slot, 4 * part : 4 * part + 4], axis=0, keepdims=True)
            for part in (0, 1)
            for slot in range(src_count)
        ],
        axis=0,
    )
    sums = jnp.sum(rows, axis=1, keepdims=True)
    lane = lax.broadcasted_iota(jnp.int32, (src_count, src_count), 1)
    row = lax.broadcasted_iota(jnp.int32, (src_count, src_count), 0)
    for part in (0, 1):
        picked = jnp.where(lane == row, sums[part * src_count : (part + 1) * src_count], 0.0)
        out_ref[0, part, 0] = jnp.sum(picked, axis=0, keepdims=True)

    wait_bytes(result.at[p, pl.ds(0, blocks - 1)], gone)

    @each(0, src_count)
    def _(slot):
        @pl.when(jnp.logical_and(slot != p, count(slot, p) > 0))
        def _():
            wait_bytes(result.at[slot, pl.ds(0, blocks)], gone)
            wait_bytes(result.at[slot, pl.ds(0, blocks - 1)], gone)


def on_device(sizes, perambulator, elemental, source_order, column_order):
    operators = elemental.shape[0]
    eigen = elemental.shape[-1]
    _, slots, _, block_cols, components = perambulator.shape
    src_count, col_count, half_count = sizes
    blocks = col_count * half_count
    spins = components // eigen
    sem = pltpu.SemaphoreType.DMA
    flag = pltpu.SemaphoreType.REGULAR
    return pl.pallas_call(
        functools.partial(kernel, sizes),
        out_shape=pltpu.VMEM((1, 2, operators, operators, slots), jnp.float32),
        in_specs=[pl.BlockSpec(memory_space=pl.ANY)] * 4,
        out_specs=pl.BlockSpec(memory_space=pltpu.VMEM),
        scratch_shapes=[
            pltpu.VMEM((slots, 2, block_cols, components), jnp.bfloat16),
            pltpu.VMEM((2, eigen, eigen), jnp.bfloat16),
            pltpu.SMEM((slots,), jnp.int32),
            pltpu.VMEM((1, eigen), jnp.int32),
            pltpu.VMEM((slots, spins, 2, block_cols, eigen), jnp.bfloat16),
            pltpu.VMEM((slots, 2, eigen, eigen), jnp.bfloat16),
            pltpu.VMEM((2 * block_cols, 2 * eigen), jnp.bfloat16),
            pltpu.VMEM((slots, blocks, 2, block_cols, eigen), jnp.bfloat16),
            pltpu.VMEM((slots, blocks, 2, block_cols, block_cols), jnp.bfloat16),
            pltpu.VMEM((slots, 8, block_cols), jnp.float32),
            pltpu.VMEM((slots, 2 * blocks, 8, block_cols), jnp.float32),
            pltpu.VMEM((slots, 8, block_cols), jnp.float32),
            sem,
            sem((slots, 3)),
            sem((slots,)),
            sem((slots,)),
            sem((slots,)),
            flag((slots,)),
        ],
        compiler_params=pltpu.CompilerParams(collective_id=0, has_side_effects=True),
    )(perambulator, elemental, source_order, column_order)


def solution(mesh):
    sizes = (mesh.shape["src"], mesh.shape["col"], mesh.shape["half"])
    return jax.shard_map(
        functools.partial(on_device, sizes),
        mesh=mesh,
        in_specs=(
            P(("cfg", "src"), None, None, ("col", "half"), None),
            P(None, ("cfg", "src"), None, None, None),
            P("cfg"),
            P(("cfg", "src"), None),
        ),
        out_specs=P(("cfg", "src"), None, None, None, None),
        check_vma=False,
    )
```

```python
import functools

import jax
import jax.numpy as jnp
from jax import lax
from jax.experimental import pallas as pl
from jax.experimental.pallas import tpu as pltpu
from jax.sharding import PartitionSpec as P

spin_sign = (1.0, 1.0, -1.0, -1.0)
MESH = pl.DeviceIdType.MESH
NT = (((1,), (1,)), ((), ()))


def dot_nt(a, b):
    return lax.dot_general(a, b, NT, preferred_element_type=jnp.float32)


def kernel(
    sizes,
    tiles_hbm, elem_hbm, order_hbm, column_hbm,
    out_ref,
    tiles, elem, order, column,
    near, coef, left, mirror, forward, partial, result, total,
    gone, tile_recv, coef_recv, share_recv, result_recv, above,
):
    src_count, col_count, half_count = sizes
    blocks = col_count * half_count
    half = blocks // 2
    block_cols, components = tiles.shape[2], tiles.shape[3]
    eigen = elem.shape[-1]
    spins = components // eigen
    piece = eigen // blocks
    last = src_count - 1
    p = lax.axis_index("src")
    b = lax.axis_index("col") * half_count + lax.axis_index("half")
    offsets = [2 * j if j < half else 2 * (j - half) + 1 for j in range(blocks)]
    each = functools.partial(pl.loop, unroll=src_count <= 8)

    def device(slot, block):
        return {
            "src": slot,
            "col": lax.div(block, half_count),
            "half": lax.rem(block, half_count),
        }

    def signal(sem, slot, block):
        pl.semaphore_signal(sem, inc=1, device_id=device(slot, block), device_id_type=MESH)

    def send(src, dst, recv_sem, slot, block):
        pltpu.make_async_remote_copy(
            src_ref=src, dst_ref=dst, send_sem=gone, recv_sem=recv_sem,
            device_id=device(slot, block), device_id_type=MESH,
        ).start()

    def wait_bytes(ref, sem):
        pltpu.make_async_copy(ref, ref, sem).wait()

    def shifted(block, offset):
        return lax.rem(block + offset + blocks, blocks)

    def spin_of(block):
        if isinstance(block, int):
            return block * block_cols // eigen
        return lax.div(block * block_cols, eigen)

    def sign_of(block):
        return jnp.where(spin_of(block) < 2, spin_sign[0], spin_sign[2]).astype(jnp.float32)

    def rows_of(block):
        if isinstance(block, int):
            return pl.ds(block * block_cols % eigen, block_cols)
        return pl.ds(pl.multiple_of(lax.rem(block * block_cols, eigen), block_cols), block_cols)

    def upward(low, high):
        whole = jnp.where(jnp.logical_or(lax.rem(high, 2) == 0, high - low == 1), blocks, 0)
        return jnp.where(high == 1, half, whole)

    def count(source, target):
        n = upward(jnp.minimum(source, target), jnp.maximum(source, target))
        return jnp.where(source < target, n, blocks - n)

    def goes(source, target, j):
        n = upward(jnp.minimum(source, target), jnp.maximum(source, target))
        return jnp.where(source < target, j < n, j >= n)

    barrier = pltpu.get_barrier_semaphore()

    for k in range(1, blocks):
        signal(barrier, p, shifted(b, k))

    @each(0, src_count)
    def _(slot):
        @pl.when(slot > p)
        def _():
            for k in range(blocks):
                signal(barrier, slot, k)

    loads = [
        pltpu.make_async_copy(elem_hbm.at[0, 0], elem, coef_recv.at[p]),
        pltpu.make_async_copy(column_hbm, column, share_recv.at[p]),
        pltpu.make_async_copy(order_hbm, order, tile_recv.at[p, 2]),
        pltpu.make_async_copy(tiles_hbm.at[0], tiles, tile_recv.at[p, 1]),
    ]
    for load in loads:
        load.start()

    first_column = b < half_count

    def greet():
        pl.semaphore_wait(barrier, blocks - 1 + p * blocks)

        @each(0, src_count)
        def _(slot):
            @pl.when(slot < p)
            def _():
                signal(above.at[p], slot, b)

    pl.when(jnp.logical_not(first_column))(greet)

    loads[0].wait()
    loads[1].wait()
    pick = (
        lax.broadcasted_iota(jnp.int32, (eigen, eigen), 0) == column[...]
    ).astype(jnp.float32).T.astype(jnp.bfloat16)
    both = jnp.concatenate([elem[0], elem[1]], axis=1)
    picked = jnp.dot(pick, both, preferred_element_type=jnp.float32).astype(jnp.bfloat16)
    coef[p, 0] = picked[:, :eigen]
    coef[p, 1] = picked[:, eigen:]

    loads[2].wait()
    loads[3].wait()
    pl.when(first_column)(greet)

    def sort(slot):
        for spin in range(spins):
            near[slot, spin] = tiles[order[slot], :, :, spin * eigen : (spin + 1) * eigen]

    my_piece = pl.ds(pl.multiple_of(b * piece, piece), piece)

    def relayed(source, target):
        return (target == 0) & (source > 1) & (count(source, 1) > 0)

    def send_coef(slot):
        @pl.when((count(p, slot) > 0) & jnp.logical_not(relayed(p, slot)))
        def _():
            send(
                coef.at[p, :, my_piece, :], coef.at[p, :, my_piece, :],
                coef_recv.at[p], slot, b,
            )

    groups = [(0, half), (half, blocks - 1), (blocks - 1, blocks)]

    def group_of(j):
        return [start <= j < stop for start, stop in groups].index(True)

    def offset_of(j):
        return offsets[j]

    def send_unit(slot, j):
        @pl.when(goes(p, slot, j))
        def _():
            block = jnp.where(p < slot, shifted(b, offset_of(j)), shifted(b, -offset_of(j)))
            send(
                near.at[slot, spin_of(block)], mirror.at[p, b],
                tile_recv.at[p, group_of(j)], slot, block,
            )

    def send_units(slot, start, stop):
        for j in range(start, stop):
            send_unit(slot, j)

    @each(0, src_count)
    def _(slot):
        @pl.when(slot < p)
        def _():
            send_coef(slot)

    @each(0, src_count)
    def _(slot):
        @pl.when(slot < p)
        def _():
            sort(slot)
            send_units(slot, 0, 1)

    for j in range(1, blocks):
        @each(0, src_count)
        def _(slot):
            @pl.when(slot < p)
            def _():
                send_units(slot, j, j + 1)

    @each(0, src_count)
    def _(slot):
        @pl.when(slot >= p)
        def _():
            sort(slot)

    @pl.when(p < last)
    def _():
        pl.semaphore_wait(above.at[p + 1], 1)
        send_coef(p + 1)
        send_units(p + 1, 0, 1)

        @pl.when(p == 0)
        def _():
            send_units(p + 1, 1, blocks)


    @each(0, src_count)
    def _(slot):
        @pl.when(slot > p + 1)
        def _():
            pl.semaphore_wait(above.at[slot], 1)
            send_coef(slot)
            send_units(slot, 0, blocks)

    @pl.when(jnp.logical_and(p > 0, p < last))
    def _():
        send_units(p + 1, 1, blocks)

    def others(act):
        @each(0, src_count)
        def _(slot):
            @pl.when(slot != p)
            def _():
                act(slot)

    def share_coef(slot):
        @pl.when(count(slot, p) > 0)
        def _():
            wait_bytes(coef.at[slot, :, pl.ds(0, piece), :], coef_recv.at[slot])

            @pl.when((p == 1) & (count(slot, 0) > 0) & relayed(slot, 0))
            def _():
                send(
                    coef.at[slot, :, my_piece, :], coef.at[slot, :, my_piece, :],
                    coef_recv.at[slot], 0, b,
                )

            for k in range(1, blocks):
                send(
                    coef.at[slot, :, my_piece, :], coef.at[slot, :, my_piece, :],
                    share_recv.at[slot], p, shifted(b, k),
                )

    def diag_source(k):
        return b >= half if k == half else b >= 0

    def diag_target(k):
        return b < half if k == half else b >= 0

    for k in range(1, half + 1):
        @pl.when(diag_source(k))
        def _():
            block = shifted(b, -k)
            send(
                near.at[p, spin_of(block)], mirror.at[p, b],
                tile_recv.at[p, 0], p, block,
            )

    own_real, own_imag = coef[p, 0, rows_of(b), :], coef[p, 1, rows_of(b), :]
    left[:block_cols, :eigen] = own_real
    left[:block_cols, eigen:] = -own_imag
    left[block_cols:, :eigen] = own_imag
    left[block_cols:, eigen:] = own_real

    def make_forward(slot, block):
        far_real, far_imag = coef[slot, 0, rows_of(block), :], coef[slot, 1, rows_of(block), :]
        mine = jnp.concatenate([near[slot, spin_of(block), 0], near[slot, spin_of(block), 1]], axis=1)
        real = jnp.concatenate([far_real, -far_imag], axis=1)
        imag = jnp.concatenate([far_imag, far_real], axis=1)
        product = dot_nt(jnp.concatenate([real, imag], axis=0), mine).astype(jnp.bfloat16)
        forward[slot, block, 0] = product[:block_cols]
        forward[slot, block, 1] = product[block_cols:]

    def fold(value):
        return jnp.sum(value.reshape(block_cols // 8, 8, block_cols), axis=0)

    def multiply(slot, block, away, weight, first):
        backward = dot_nt(jnp.concatenate([away[0], away[1]], axis=1), left[...])
        backward = backward.astype(jnp.bfloat16).astype(jnp.float32)
        br, bi = backward[:, :block_cols], backward[:, block_cols:]
        fr = forward[slot, block, 0].astype(jnp.float32)
        fi = forward[slot, block, 1].astype(jnp.float32)
        scale = weight * sign_of(block) * sign_of(b)
        real = scale * fold(fr * br - fi * bi)
        imag = scale * fold(fr * bi + fi * br)
        packed = jnp.concatenate([real[:4] + real[4:], imag[:4] + imag[4:]], axis=0)
        if first:
            partial[slot] = packed
        else:
            partial[slot] += packed

    def by_column(j):
        return jnp.where(lax.rem(b, 2) == 0, j, j ^ 1)

    def share_result(slot):
        for j in range(blocks):
            block = by_column(j)

            @pl.when(block != b)
            def _():
                send(result.at[slot, b], result.at[slot, b], result_recv.at[slot], p, block)

    def send_result(slot):
        for j in range(blocks):
            send(
                result.at[slot, b], result.at[p, blocks + b],
                result_recv.at[p], slot, by_column(j),
            )

    make_forward(p, b)
    multiply(p, b, near[p, spin_of(b)], 1.0, True)
    for k in range(1, half + 1):
        @pl.when(diag_target(k))
        def _():
            make_forward(p, shifted(b, k))

    @each(0, src_count)
    def _(step):
        @pl.when(step < p)
        def _():
            share_coef(p - 1 - step)

    @each(0, src_count)
    def _(slot):
        @pl.when(slot > p)
        def _():
            share_coef(slot)


    def take_diagonal():
        for n in (half - 1, half):
            @pl.when(diag_target(half) == (n == half))
            def _():
                wait_bytes(mirror.at[p, pl.ds(0, n)], tile_recv.at[p, 0])

        for k in range(1, half + 1):
            @pl.when(diag_target(k))
            def _():
                block = shifted(b, k)
                multiply(p, block, mirror[p, block], 2.0, False)
        result[p, b] = partial[p]
        share_result(p)

    def source_block(slot, j):
        return jnp.where(slot < p, shifted(b, -offset_of(j)), shifted(b, offset_of(j)))

    def prepare(slot):
        @pl.when(count(slot, p) > 0)
        def _():
            wait_bytes(coef.at[slot, :, pl.ds(0, eigen - piece), :], share_recv.at[slot])
            partial[slot] = jnp.zeros(partial.shape[1:], jnp.float32)
            for block in range(blocks):
                make_forward(slot, block)

    def take_units(slot, start, stop):
        @pl.when(goes(slot, p, start))
        def _():
            wait_bytes(mirror.at[slot, pl.ds(0, stop - start)], tile_recv.at[slot, group_of(start)])
            for j in range(start, stop):
                block = source_block(slot, j)
                multiply(slot, block, mirror[slot, block], 1.0, False)

    def finish(slot):
        @pl.when(count(slot, p) > 0)
        def _():
            result[slot, b] = partial[slot]

            @pl.when(slot < p)
            def _():
                send_result(slot)

            share_result(slot)

            @pl.when(slot > p)
            def _():
                send_result(slot)

    def take_all(slot):
        for start, stop in groups:
            take_units(slot, start, stop)
        finish(slot)

    @each(0, src_count)
    def _(slot):
        @pl.when(slot != p)
        def _():
            prepare(slot)
            take_all(slot)

        @pl.when(slot == jnp.where(p == 0, 1, 0))
        def _():
            take_diagonal()

    for k in range(1, half + 1):
        @pl.when(diag_source(k))
        def _():
            wait_bytes(mirror.at[p, 0], gone)

    @each(0, src_count)
    def _(slot):
        @pl.when(slot != p)
        def _():
            sent, received = count(p, slot), count(slot, p)

            @pl.when((sent > 0) & jnp.logical_not(relayed(p, slot)))
            def _():
                wait_bytes(coef.at[slot, :, pl.ds(0, piece), :], gone)

            @pl.when((p == 1) & (received > 0) & (count(slot, 0) > 0) & relayed(slot, 0))
            def _():
                wait_bytes(coef.at[slot, :, pl.ds(0, piece), :], gone)

            for n in range(1, blocks + 1):
                @pl.when(sent == n)
                def _():
                    wait_bytes(mirror.at[slot, pl.ds(0, n)], gone)

            @pl.when(received > 0)
            def _():
                wait_bytes(coef.at[slot, :, pl.ds(0, eigen - piece), :], gone)

    @each(0, src_count)
    def _(slot):
        here = jnp.logical_or(slot == p, count(slot, p) > 0)
        there = jnp.logical_and(slot != p, count(p, slot) > 0)
        expected = jnp.where(here, blocks - 1, 0) + jnp.where(there, blocks, 0)
        for n in (blocks - 1, blocks, 2 * blocks - 1):
            @pl.when(expected == n)
            def _():
                wait_bytes(result.at[slot, pl.ds(0, n)], result_recv.at[slot])

        total[slot] = jnp.zeros(total.shape[1:], jnp.float32)

        @pl.when(jnp.logical_or(slot == p, count(slot, p) > 0))
        def _():
            total[slot] += jnp.sum(result[slot, :blocks], axis=0)

        @pl.when(jnp.logical_and(slot != p, count(p, slot) > 0))
        def _():
            total[slot] += jnp.sum(result[slot, blocks:], axis=0)

    rows = jnp.concatenate(
        [
            jnp.sum(total[slot, 4 * part : 4 * part + 4], axis=0, keepdims=True)
            for part in (0, 1)
            for slot in range(src_count)
        ],
        axis=0,
    )
    sums = jnp.sum(rows, axis=1, keepdims=True)
    lane = lax.broadcasted_iota(jnp.int32, (src_count, src_count), 1)
    row = lax.broadcasted_iota(jnp.int32, (src_count, src_count), 0)
    for part in (0, 1):
        picked = jnp.where(lane == row, sums[part * src_count : (part + 1) * src_count], 0.0)
        out_ref[0, part, 0] = jnp.sum(picked, axis=0, keepdims=True)

    wait_bytes(result.at[p, pl.ds(0, blocks - 1)], gone)

    @each(0, src_count)
    def _(slot):
        @pl.when(jnp.logical_and(slot != p, count(slot, p) > 0))
        def _():
            wait_bytes(result.at[slot, pl.ds(0, blocks)], gone)
            wait_bytes(result.at[slot, pl.ds(0, blocks - 1)], gone)


def on_device(sizes, perambulator, elemental, source_order, column_order):
    operators = elemental.shape[0]
    eigen = elemental.shape[-1]
    _, slots, _, block_cols, components = perambulator.shape
    src_count, col_count, half_count = sizes
    blocks = col_count * half_count
    spins = components // eigen
    sem = pltpu.SemaphoreType.DMA
    flag = pltpu.SemaphoreType.REGULAR
    return pl.pallas_call(
        functools.partial(kernel, sizes),
        out_shape=pltpu.VMEM((1, 2, operators, operators, slots), jnp.float32),
        in_specs=[pl.BlockSpec(memory_space=pl.ANY)] * 4,
        out_specs=pl.BlockSpec(memory_space=pltpu.VMEM),
        scratch_shapes=[
            pltpu.VMEM((slots, 2, block_cols, components), jnp.bfloat16),
            pltpu.VMEM((2, eigen, eigen), jnp.bfloat16),
            pltpu.SMEM((slots,), jnp.int32),
            pltpu.VMEM((1, eigen), jnp.int32),
            pltpu.VMEM((slots, spins, 2, block_cols, eigen), jnp.bfloat16),
            pltpu.VMEM((slots, 2, eigen, eigen), jnp.bfloat16),
            pltpu.VMEM((2 * block_cols, 2 * eigen), jnp.bfloat16),
            pltpu.VMEM((slots, blocks, 2, block_cols, eigen), jnp.bfloat16),
            pltpu.VMEM((slots, blocks, 2, block_cols, block_cols), jnp.bfloat16),
            pltpu.VMEM((slots, 8, block_cols), jnp.float32),
            pltpu.VMEM((slots, 2 * blocks, 8, block_cols), jnp.float32),
            pltpu.VMEM((slots, 8, block_cols), jnp.float32),
            sem,
            sem((slots, 3)),
            sem((slots,)),
            sem((slots,)),
            sem((slots,)),
            flag((slots,)),
        ],
        compiler_params=pltpu.CompilerParams(collective_id=0, has_side_effects=True),
    )(perambulator, elemental, source_order, column_order)


def solution(mesh):
    sizes = (mesh.shape["src"], mesh.shape["col"], mesh.shape["half"])
    return jax.shard_map(
        functools.partial(on_device, sizes),
        mesh=mesh,
        in_specs=(
            P(("cfg", "src"), None, None, ("col", "half"), None),
            P(None, ("cfg", "src"), None, None, None),
            P("cfg"),
            P(("cfg", "src"), None),
        ),
        out_specs=P(("cfg", "src"), None, None, None, None),
        check_vma=False,
    )
```
